32 devices in a mesh: dx: 4 (over y, x), dy: 8 (over z, core).
Axes of the slice: x: 2, y: 2, z: 4, core: 2. Of those that a mesh axis runs over, the one named last changes fastest.
Arguments:
- fine_nodes: bfloat16 [128, 128, 512], P('dx', 'dy'), may hold values from -6 to 6
- fine_edges: bfloat16 [6, 128, 128, 512], P(None, 'dx', 'dy'), may hold values from -6 to 6
- fine_links: int32 [6, 128, 128], P(None, 'dx', 'dy'), may hold values from 0 to 48
- mid_nodes: bfloat16 [32, 32, 512], P('dx', 'dy'), may hold values from -6 to 6
- mid_edges: bfloat16 [6, 32, 32, 512], P(None, 'dx', 'dy'), may hold values from -6 to 6
- mid_links: int32 [6, 32, 32], P(None, 'dx', 'dy'), may hold values from 0 to 8
- coarse_nodes: bfloat16 [8, 8, 512], replicated, may hold values from -6 to 6
- coarse_edges: bfloat16 [6, 8, 8, 512], replicated, may hold values from -6 to 6
- coarse_links: int32 [6, 8, 8], replicated, may hold values from 0 to 63
- edge_self: bfloat16 [1, 512, 1536], replicated, may hold values from -0.25 to 0.25
- edge_sender: bfloat16 [1, 512, 1536], replicated, may hold values from -0.25 to 0.25
- edge_receiver: bfloat16 [1, 512, 1536], replicated, may hold values from -0.25 to 0.25
- edge_bias: float32 [1, 1536], replicated, may hold values from -6 to 6
- edge_output: bfloat16 [1, 1536, 512], replicated, may hold values from -0.15625 to 0.15625
- edge_gain: float32 [1, 512], replicated, may hold values from 0.1 to 1.9
- edge_shift: float32 [1, 512], replicated, may hold values from -3 to 3
- node_self: bfloat16 [1, 512, 1536], replicated, may hold values from -0.25 to 0.25
- node_summed: bfloat16 [1, 512, 1536], replicated, may hold values from -0.109375 to 0.109375
- node_bias: float32 [1, 1536], replicated, may hold values from -6 to 6
- node_output: bfloat16 [1, 1536, 512], replicated, may hold values from -0.15625 to 0.15625
- node_gain: float32 [1, 512], replicated, may hold values from 0.1 to 1.9
- node_shift: float32 [1, 512], replicated, may hold values from -3 to 3
- prolongation: bfloat16 [1, 512, 512], replicated, may hold values from -0.25 to 0.25
- pooling: bfloat16 [1, 512, 512], replicated, may hold values from -0.25 to 0.25
Outputs:
- fine_out: bfloat16 [128, 128, 512], P('dx', 'dy')
- fine_edges_out: bfloat16 [6, 128, 128, 512], P(None, 'dx', 'dy')
- mid_out: bfloat16 [32, 32, 512], P('dx', 'dy')
- mid_edges_out: bfloat16 [6, 32, 32, 512], P(None, 'dx', 'dy')
- coarse_out: bfloat16 [8, 8, 512], replicated
- coarse_edges_out: bfloat16 [6, 8, 8, 512], replicated
The draws below stay inside these ranges and needn't reach their ends.
Inputs may be any that keep to these rules, and one draw needn't show every extreme that they name: `fine_links`: code q names the sender at offset (q // 7 - 3, q % 7 - 3) from the receiver. `mid_links`: code q names the sender at offset (q // 3 - 1, q % 3 - 1) from the receiver.
All inputs are finite; a program needn't handle non-finite values.
Results may differ from the reference program's by a relative error of at most 0.012.
Values may be sent and summed in bfloat16 or wider, within the bound.
A program may use at most 128 MiB of HBM per device.

```python
import math
import jax
import jax.numpy as jnp
from jax import lax

D = 512
HIDDEN_SIZE = 1536
FANOUT = 6
FINE_REACH = 3
MID_REACH = 1
LAYERS = 1
NX = 128
NY = 128
MX = 32
MY = 32
CX = 8
CY = 8


def place_ends(values, rng, smallest, top_value):
    dims = values.shape
    index_at = [jax.random.randint(jax.random.fold_in(rng, axis), (), 0, dims[axis]) for axis in range(len(dims))]
    values = values.at[tuple(index_at)].set(smallest)
    longest = dims.index(max(dims))
    index_at[longest] = (index_at[longest] + 1) % dims[longest]
    return values.at[tuple(index_at)].set(top_value)


def level_of(stream_key, dims, pieces, least, largest):
    def one(dim, parts):
        steps = jax.random.uniform(jax.random.fold_in(jax.random.fold_in(stream_key, 6), dim), (parts,), jnp.float32, least / len(pieces), largest / len(pieces))
        return jnp.repeat(jnp.exp(steps), dims[dim] // parts).reshape((-1,) + (1,) * (len(dims) - dim - 1))

    factor_of = one(*pieces[0])
    for cut in pieces[1:]:
        factor_of = factor_of * one(*cut)
    return factor_of


def normal_values(own_key, dims, scale, bound, split=(), dtype=jnp.bfloat16):
    factor_of = level_of(own_key, dims, split, -0.22, 0.18) if split else 1.0
    entries = jax.random.normal(own_key, dims, jnp.float32) * scale * factor_of
    return jnp.minimum(jnp.maximum(entries, -bound), bound).astype(dtype)


def setup_inputs(seed: int = 0) -> dict:
    splits = jax.random.split(jax.random.key(seed), 25)
    return {
        "fine_nodes": normal_values(splits[0], (NX, NY, D), 1.0, 6.0, ((0, 4), (1, 8))),
        "fine_edges": normal_values(splits[1], (FANOUT, NX, NY, D), 1.0, 6.0, ((1, 4), (2, 8))),
        "fine_links": place_ends(jax.random.randint(splits[2], (FANOUT, NX, NY), 0, (2 * FINE_REACH + 1) ** 2), jax.random.fold_in(splits[2], 1), 0, ((2 * FINE_REACH + 1) ** 2) - 1).astype(jnp.int32),
        "mid_nodes": normal_values(splits[3], (MX, MY, D), 1.0, 6.0, ((0, 4), (1, 8))),
        "mid_edges": normal_values(splits[4], (FANOUT, MX, MY, D), 1.0, 6.0, ((1, 4), (2, 8))),
        "mid_links": place_ends(jax.random.randint(splits[5], (FANOUT, MX, MY), 0, (2 * MID_REACH + 1) ** 2), jax.random.fold_in(splits[5], 1), 0, ((2 * MID_REACH + 1) ** 2) - 1).astype(jnp.int32),
        "coarse_nodes": normal_values(splits[6], (CX, CY, D), 1.0, 6.0),
        "coarse_edges": normal_values(splits[7], (FANOUT, CX, CY, D), 1.0, 6.0),
        "coarse_links": place_ends(jax.random.randint(splits[8], (FANOUT, CX, CY), 0, CX * CY), jax.random.fold_in(splits[8], 1), 0, (CX * CY) - 1).astype(jnp.int32),
        "edge_self": normal_values(splits[9], (LAYERS, D, HIDDEN_SIZE), D ** -0.5, 0.25),
        "edge_sender": normal_values(splits[10], (LAYERS, D, HIDDEN_SIZE), D ** -0.5, 0.25),
        "edge_receiver": normal_values(splits[11], (LAYERS, D, HIDDEN_SIZE), D ** -0.5, 0.25),
        "edge_bias": normal_values(splits[12], (LAYERS, HIDDEN_SIZE), 1.0, 6.0, (), jnp.float32),
        "edge_output": normal_values(splits[13], (LAYERS, HIDDEN_SIZE, D), HIDDEN_SIZE ** -0.5, 0.15625),
        "edge_gain": jnp.clip(1.0 + 0.18 * jax.random.normal(splits[14], (LAYERS, D), jnp.float32), 0.1, 1.9),
        "edge_shift": normal_values(splits[15], (LAYERS, D), 0.5, 3.0, (), jnp.float32),
        "node_self": normal_values(splits[16], (LAYERS, D, HIDDEN_SIZE), D ** -0.5, 0.25),
        "node_summed": normal_values(splits[17], (LAYERS, D, HIDDEN_SIZE), (FANOUT * D) ** -0.5, 0.109375),
        "node_bias": normal_values(splits[18], (LAYERS, HIDDEN_SIZE), 1.0, 6.0, (), jnp.float32),
        "node_output": normal_values(splits[19], (LAYERS, HIDDEN_SIZE, D), HIDDEN_SIZE ** -0.5, 0.15625),
        "node_gain": jnp.clip(1.0 + 0.18 * jax.random.normal(splits[20], (LAYERS, D), jnp.float32), 0.1, 1.9),
        "node_shift": normal_values(splits[21], (LAYERS, D), 0.5, 3.0, (), jnp.float32),
        "prolongation": normal_values(splits[22], (LAYERS, D, D), D ** -0.5, 0.25),
        "pooling": normal_values(splits[23], (LAYERS, D, D), D ** -0.5, 0.25),
    }


epsilon = 1e-05

def normalize(values, gain_term, shift_term):
    average = lax.optimization_barrier(jnp.mean(values, axis=-1, keepdims=True))
    centred = values - average
    variance = lax.optimization_barrier(jnp.mean(centred * centred, axis=-1, keepdims=True))
    return centred * lax.rsqrt(variance + epsilon) * gain_term + shift_term

def level_update(nodes, edges, sender_terms, senders, weights):
    self_matrix, receiver_matrix, edge_bias, edge_output, edge_gain, edge_shift, node_self, node_summed, node_bias, node_output, node_gain, node_shift = weights
    fanout, height, breadth, feature = edges.shape
    places = height * breadth
    flat_nodes = nodes.reshape(places, feature)
    flat_edges = edges.reshape(fanout * places, feature)
    receiver = jnp.dot(flat_nodes, receiver_matrix, preferred_element_type=jnp.float32) + edge_bias
    latent = jnp.dot(flat_edges, self_matrix, preferred_element_type=jnp.float32).reshape(fanout, places, -1)
    latent = latent + jnp.take(sender_terms, senders.reshape(fanout, places), axis=0) + receiver[None]
    hidden = jax.nn.silu(latent).astype(jnp.bfloat16).reshape(fanout * places, -1)
    message = jnp.dot(hidden, edge_output, preferred_element_type=jnp.float32)
    new_edges = (flat_edges.astype(jnp.float32) + normalize(message, edge_gain, edge_shift)).astype(jnp.bfloat16)
    new_edges = new_edges.reshape(fanout, places, feature)
    summed = lax.optimization_barrier(jnp.sum(new_edges.astype(jnp.float32), axis=0)).astype(jnp.bfloat16)
    node_hidden = jnp.dot(flat_nodes, node_self, preferred_element_type=jnp.float32)
    node_hidden = node_hidden + jnp.dot(summed, node_summed, preferred_element_type=jnp.float32) + node_bias
    node_hidden = jax.nn.silu(node_hidden).astype(jnp.bfloat16)
    node_message = jnp.dot(node_hidden, node_output, preferred_element_type=jnp.float32)
    new_nodes = (flat_nodes.astype(jnp.float32) + normalize(node_message, node_gain, node_shift)).astype(jnp.bfloat16)
    return (new_nodes.reshape(height, breadth, feature), new_edges.reshape(fanout, height, breadth, feature))

def blocked_update(nodes, edges, sender_terms, senders, weights):
    height, breadth, feature = nodes.shape
    fanout = edges.shape[0]
    block = math.gcd(height, 8)
    groups = height // block
    node_blocks = nodes.reshape(groups, block, breadth, feature)
    edge_blocks = edges.reshape(fanout, groups, block, breadth, feature).transpose(1, 0, 2, 3, 4)
    index_blocks = senders.reshape(fanout, groups, block, breadth).transpose(1, 0, 2, 3)
    new_nodes, new_edges = lax.map(lambda block_items: level_update(block_items[0], block_items[1], sender_terms, block_items[2], weights), (node_blocks, edge_blocks, index_blocks))
    new_nodes = new_nodes.reshape(height, breadth, feature)
    new_edges = new_edges.transpose(1, 0, 2, 3, 4).reshape(fanout, height, breadth, feature)
    return (new_nodes, new_edges)

def offset_index(link_codes, reach_cells, padded_breadth):
    window_span = 2 * reach_cells + 1
    row_place = lax.broadcasted_iota(jnp.int32, link_codes.shape, 1)
    col_place = lax.broadcasted_iota(jnp.int32, link_codes.shape, 2)
    return ((row_place + link_codes // window_span) * padded_breadth + col_place + link_codes % window_span).astype(jnp.int32)

def widen(parent_values, height, breadth):
    parent_rows, parent_cols, feature = parent_values.shape
    spread_out = jnp.broadcast_to(parent_values[:, None, :, None, :], (parent_rows, 4, parent_cols, 4, feature))
    return spread_out.reshape(height, breadth, feature)

def reference(fine_nodes, fine_edges, fine_links, mid_nodes, mid_edges, mid_links, coarse_nodes, coarse_edges, coarse_links, edge_self, edge_sender, edge_receiver, edge_bias, edge_output, edge_gain, edge_shift, node_self, node_summed, node_bias, node_output, node_gain, node_shift, prolongation, pooling):
    fine_rows, fine_cols, feature = fine_nodes.shape
    mid_rows, mid_cols = (mid_nodes.shape[0], mid_nodes.shape[1])
    coarse_rows, coarse_cols = (coarse_nodes.shape[0], coarse_nodes.shape[1])
    for layer_index in range(edge_self.shape[0]):
        weights = tuple((stacked[layer_index] for stacked in (edge_self, edge_receiver, edge_bias, edge_output, edge_gain, edge_shift, node_self, node_summed, node_bias, node_output, node_gain, node_shift)))
        sender_matrix = edge_sender[layer_index]
        padded = jnp.pad(fine_nodes, ((FINE_REACH, FINE_REACH), (FINE_REACH, FINE_REACH), (0, 0)), mode='wrap')
        fine_terms = jnp.dot(padded.reshape(-1, feature), sender_matrix, preferred_element_type=jnp.float32)
        fine_index = offset_index(fine_links, FINE_REACH, fine_cols + 2 * FINE_REACH)
        fine_new, fine_edges = blocked_update(fine_nodes, fine_edges, fine_terms, fine_index, weights)
        pooled = mid_nodes.astype(jnp.float32).reshape(coarse_rows, 4, coarse_cols, 4, feature).mean(axis=(1, 3)).astype(jnp.bfloat16)
        raised = jnp.dot(pooled.reshape(-1, feature), pooling[layer_index], preferred_element_type=jnp.float32)
        coarse_nodes = (coarse_nodes.astype(jnp.float32) + raised.reshape(coarse_rows, coarse_cols, feature)).astype(jnp.bfloat16)
        coarse_terms = jnp.dot(coarse_nodes.reshape(-1, feature), sender_matrix, preferred_element_type=jnp.float32)
        coarse_nodes, coarse_edges = blocked_update(coarse_nodes, coarse_edges, coarse_terms, coarse_links, weights)
        lifted = jnp.dot(coarse_nodes.reshape(-1, feature), prolongation[layer_index], preferred_element_type=jnp.float32)
        lifted = lifted.reshape(coarse_rows, coarse_cols, feature)
        mid_nodes = (mid_nodes.astype(jnp.float32) + widen(lifted, mid_rows, mid_cols)).astype(jnp.bfloat16)
        padded = jnp.pad(mid_nodes, ((MID_REACH, MID_REACH), (MID_REACH, MID_REACH), (0, 0)), mode='wrap')
        mid_terms = jnp.dot(padded.reshape(-1, feature), sender_matrix, preferred_element_type=jnp.float32)
        mid_index = offset_index(mid_links, MID_REACH, mid_cols + 2 * MID_REACH)
        mid_nodes, mid_edges = blocked_update(mid_nodes, mid_edges, mid_terms, mid_index, weights)
        lifted_mid = jnp.dot(mid_nodes.reshape(-1, feature), prolongation[layer_index], preferred_element_type=jnp.float32)
        lifted_mid = lifted_mid.reshape(mid_rows, mid_cols, feature)
        fine_nodes = (fine_new.astype(jnp.float32) + widen(lifted_mid, fine_rows, fine_cols)).astype(jnp.bfloat16)
    return (fine_nodes, fine_edges, mid_nodes, mid_edges, coarse_nodes, coarse_edges)
```

```python
import functools

import jax
import jax.numpy as jnp
from jax import lax
from jax.experimental import pallas as pl
from jax.experimental.pallas import tpu as pltpu
from jax.sharding import PartitionSpec as P

FINE_REACH = 3
MID_REACH = 1
BLOCK = 4
epsilon = 1e-05
F32 = jnp.float32
BF16 = jnp.bfloat16
I32 = jnp.int32


def round_up(value, unit):
    return -(-value // unit) * unit


def dot(a, b):
    return jnp.dot(a, b, preferred_element_type=F32)


def spread(values, length):
    lines, width = values.shape
    row = lax.broadcasted_iota(I32, (length, lines), 0)
    line = lax.broadcasted_iota(I32, (length, lines), 1) * width
    owner = jnp.where((row >= line) & (row < line + width), 1.0, 0.0).astype(BF16)
    rows = dot(owner, values.astype(BF16))
    row = lax.broadcasted_iota(I32, (length, width), 0)
    lane = lax.broadcasted_iota(I32, (length, width), 1)
    return jnp.sum(jnp.where(lax.rem(row, width) == lane, rows, 0.0), axis=1, keepdims=True)


def chosen(column, width):
    lane = lax.broadcasted_iota(I32, (column.shape[0], width), 1).astype(column.dtype)
    return jnp.where(column == lane, 1.0, 0.0).astype(BF16)


def front_kernel(
    across, along,
    x_hbm, mid_hbm, wrec_hbm, ws_hbm, e_hbm, ns_hbm, wsend_hbm, links_hbm, mid_links_hbm, coarse_links_hbm,
    ebias_hbm, nbias_hbm, ce_hbm, me_hbm, wo_hbm, no_hbm, nsum_hbm, pool_hbm, prol_hbm,
    x_ref, wrec_ref, e_ref, ns_ref, wsend_ref, woc_ref, noc_ref, nsum_ref, pool_ref, prol_ref, ce_ref,
    zf_ref, zc_ref, zm_ref, xns_ref, terms_ref, pick_ref, pickm_ref, pickc_ref, me_ref, midpad_ref, pooled_ref,
    mid_ref, ws_ref, links_ref, mid_links_ref, coarse_links_ref, ebias_ref, nbias_ref, mid_e_ref, wo_ref, no_ref,
    receivers, halo,
    to_left, to_right, corner_src, top, bottom, from_left, from_right, corner_dst,
    mid_src, mid_rows_dst, mid_left, mid_right, mid_corner, own_pool, pools,
    load_sem, near_send, near_recv, pool_send, pool_recv,
):
    rows, cols, feature = x_ref.shape
    mrows, mcols, _ = mid_ref.shape
    fanout, places, hidden = zf_ref.shape
    half = rows // 2
    reach = FINE_REACH
    stride = cols + 8
    total = across * along
    me_x = lax.axis_index("dx")
    me_y = lax.axis_index("dy")
    me = me_x * along + me_y
    up = lax.rem(me_x + across - 1, across)
    down = lax.rem(me_x + 1, across)
    left = lax.rem(me_y + along - 1, along)
    right = lax.rem(me_y + 1, along)

    def other(step):
        number = lax.rem(me + step, total)
        return number // along, lax.rem(number, along)

    group = fanout // 2
    loads = (
        (mid_hbm, mid_ref), (x_hbm, x_ref), (wrec_hbm, wrec_ref), (ebias_hbm, ebias_ref), (ws_hbm, ws_ref),
        (e_hbm.at[pl.ds(0, group)], e_ref.at[pl.ds(0, group)]),
        (e_hbm.at[pl.ds(group, group)], e_ref.at[pl.ds(group, group)]),
        (ns_hbm, ns_ref), (nbias_hbm, nbias_ref), (wsend_hbm, wsend_ref),
        (links_hbm, links_ref), (mid_links_hbm, mid_links_ref), (coarse_links_hbm, coarse_links_ref),
        (ce_hbm, ce_ref), (me_hbm, mid_e_ref), (wo_hbm, wo_ref), (no_hbm, no_ref), (nsum_hbm, nsum_ref),
        (pool_hbm, pool_ref), (prol_hbm, prol_ref),
    )
    loads = [pltpu.make_async_copy(source, target, load_sem.at[n]) for n, (source, target) in enumerate(loads)]
    (l_mid, l_x, l_wrec, l_ebias, l_ws, l_e0, l_e1, l_ns, l_nbias, l_wsend, l_links, l_mlinks, l_clinks,
     l_ce, l_me, l_wo, l_no, l_nsum, l_pool, l_prol) = loads
    for load in loads:
        load.start()

    barrier = pltpu.get_barrier_semaphore()

    def greet(step, carry):
        pl.semaphore_signal(barrier, inc=1, device_id=other(step), device_id_type=pl.DeviceIdType.MESH)
        return carry

    lax.fori_loop(1, total, greet, 0)

    l_mid.wait()
    mid = mid_ref[...].astype(F32)
    brows, bcols = mrows // 4, mcols // 4
    means = []
    for i in range(brows):
        strip = jnp.sum(mid[4 * i : 4 * i + 4], axis=0)
        for j in range(bcols):
            means.append(jnp.sum(strip[4 * j : 4 * j + 4], axis=0, keepdims=True) * (1.0 / 16.0))
    own_pool[...] = jnp.concatenate(means, axis=0).astype(BF16)
    mid_src[0] = jnp.concatenate([mid[i, mcols - 1 : mcols] for i in range(mrows)], axis=0).astype(BF16)
    mid_src[1] = jnp.concatenate([mid[i, 0:1] for i in range(mrows)], axis=0).astype(BF16)

    l_x.wait()
    low = lax.broadcasted_iota(I32, (half, 8, feature), 1) < 4
    first_a = x_ref[0:half, 0:8].astype(F32)
    first_b = x_ref[half:rows, 0:8].astype(F32)
    to_left[...] = jnp.where(low, first_a, pltpu.roll(first_b, 4, 1)).astype(BF16)
    last_a = x_ref[0:half, cols - 8 : cols].astype(F32)
    last_b = x_ref[half:rows, cols - 8 : cols].astype(F32)
    to_right[...] = jnp.where(low, pltpu.roll(last_a, 4, 1), last_b).astype(BF16)
    corner_src[0] = x_ref[rows - reach : rows, cols - 8 : cols]
    corner_src[1] = x_ref[rows - reach : rows, 0:8]
    corner_src[2] = x_ref[0:reach, cols - 8 : cols]
    corner_src[3] = x_ref[0:reach, 0:8]

    chunk = 512
    lanes = lambda c: pl.ds(pl.multiple_of(c * chunk, chunk), chunk)
    l_wrec.wait()
    l_ebias.wait()

    @pl.loop(0, hidden // chunk)
    def _(c):
        flat = x_ref[...].reshape(places, feature)
        receivers[:, lanes(c)] = (dot(flat, wrec_ref[:, lanes(c)]) + ebias_ref[:, lanes(c)]) * 0.5

    def own_edges(first):
        @pl.loop(0, hidden // chunk)
        def _(c):
            edges = e_ref[first : first + group].reshape(group * places, feature)
            z = dot(edges, ws_ref[:, lanes(c)]) * 0.5
            z = z.reshape(group, places, chunk) + receivers[:, lanes(c)][None]
            zf_ref[first : first + group, :, lanes(c)] = z.astype(zf_ref.dtype)

    l_ws.wait()
    l_e0.wait()
    own_edges(0)

    pl.semaphore_wait(barrier, total - 1)

    plan = (
        (to_right, from_left, (me_x, right)),
        (to_left, from_right, (me_x, left)),
        (x_ref.at[pl.ds(rows - reach, reach)], top, (down, me_y)),
        (x_ref.at[pl.ds(0, reach)], bottom, (up, me_y)),
        (corner_src.at[0], corner_dst.at[0], (down, right)),
        (corner_src.at[1], corner_dst.at[1], (down, left)),
        (corner_src.at[2], corner_dst.at[2], (up, right)),
        (corner_src.at[3], corner_dst.at[3], (up, left)),
        (mid_src.at[0], mid_left, (me_x, right)),
        (mid_src.at[1], mid_right, (me_x, left)),
        (mid_ref.at[mrows - 1], mid_rows_dst.at[0], (down, me_y)),
        (mid_ref.at[0], mid_rows_dst.at[1], (up, me_y)),
        (mid_ref.at[mrows - 1], mid_corner.at[0], (down, right)),
        (mid_ref.at[mrows - 1], mid_corner.at[1], (down, left)),
        (mid_ref.at[0], mid_corner.at[2], (up, right)),
        (mid_ref.at[0], mid_corner.at[3], (up, left)),
    )
    copies = []
    for number, (source, target, device) in enumerate(plan):
        copy = pltpu.make_async_remote_copy(
            src_ref=source, dst_ref=target, send_sem=near_send.at[number],
            recv_sem=near_recv.at[number], device_id=device, device_id_type=pl.DeviceIdType.MESH,
        )
        copy.start()
        copies.append(copy)

    def pool_copy(slot, target):
        return pltpu.make_async_remote_copy(
            src_ref=own_pool, dst_ref=pools.at[slot], send_sem=pool_send.at[slot],
            recv_sem=pool_recv.at[slot], device_id=target, device_id_type=pl.DeviceIdType.MESH,
        )

    def send_pool(step, carry):
        pool_copy(step, other(step)).start()
        return carry

    lax.fori_loop(1, total, send_pool, 0)

    l_e1.wait()
    own_edges(group)

    l_ns.wait()
    l_nbias.wait()
    l_wsend.wait()

    @pl.loop(0, hidden // chunk)
    def _(c):
        flat = x_ref[...].reshape(places, feature)
        own = (dot(flat, ns_ref[:, lanes(c)]) + nbias_ref[:, lanes(c)]) * 0.5
        xns_ref[:, lanes(c)] = own.astype(xns_ref.dtype)
        own = (dot(flat, wsend_ref[:, lanes(c)]) * 0.5).astype(BF16)
        terms_ref[reach : reach + rows, 0:cols, lanes(c)] = own.reshape(rows, cols, chunk)

    l_ce.wait()
    l_me.wait()
    for i in range(fanout * mrows):
        me_ref[i * mcols : (i + 1) * mcols, :] = mid_e_ref[i].astype(F32)

    @pl.loop(0, hidden // chunk)
    def _(c):
        zc_ref[:, lanes(c)] = (dot(ce_ref[...], ws_ref[:, lanes(c)]) * 0.5).astype(zc_ref.dtype)
        zm_ref[:, lanes(c)] = (dot(me_ref[...].astype(BF16), ws_ref[:, lanes(c)]) * 0.5).astype(zm_ref.dtype)

    rem, div = lax.rem, lax.div
    l_links.wait()
    links = links_ref[...]
    span = 2 * FINE_REACH + 1
    column = lax.broadcasted_iota(I32, links.shape, 1) + rem(links, span) + (stride - FINE_REACH)
    line = rem(lax.broadcasted_iota(I32, links.shape, 2), BLOCK) + div(links, span)
    index = line * stride + rem(column, stride)
    window = pick_ref.shape[1]
    lane = lax.broadcasted_iota(I32, (cols, window), 1)
    for s in range(rows // BLOCK):
        for k in range(fanout):
            for i in range(BLOCK):
                x = s * BLOCK + i
                hit = jnp.where(index[k, :, x : x + 1] == lane, 1.0, 0.0).astype(BF16)
                begin = ((s * fanout + k) * BLOCK + i) * cols
                pick_ref[begin : begin + cols, :] = hit

    mid_places = mrows * mcols
    l_mlinks.wait()
    l_clinks.wait()
    links = mid_links_ref[...]
    line = lax.broadcasted_iota(I32, links.shape, 2) + div(links, 3) - 1
    column = lax.broadcasted_iota(I32, links.shape, 1) + rem(links, 3) - 1
    centre = jnp.where(
        line < 0, mid_places + column,
        jnp.where(line >= mrows, mid_places + mcols + column, line * mcols + column),
    )
    side = mid_places + 2 * mcols + (line + 1) * mcols
    index = jnp.where(column < 0, side + mcols - 1, jnp.where(column >= mcols, side + (mrows + 2) * mcols, centre))
    mid_total = pickm_ref.shape[1]
    lane = lax.broadcasted_iota(I32, (mcols, mid_total), 1)
    for k in range(fanout):
        for x in range(0, mrows, 4):
            pieces = [jnp.where(index[k, :, x + i : x + i + 1] == lane, 1.0, 0.0) for i in range(4)]
            begin = (k * mrows + x) * mcols
            pickm_ref[begin : begin + 4 * mcols, :] = jnp.concatenate(pieces, axis=0).astype(BF16)
    links = coarse_links_ref[...].astype(F32)
    count = pickc_ref.shape[0]
    pickc_ref[...] = chosen(spread(links, count), pickc_ref.shape[1])

    l_wo.wait()
    l_no.wait()

    @pl.loop(0, hidden // 256)
    def _(c):
        cut = pl.ds(pl.multiple_of(c * 256, 256), 256)
        for source, target in ((wo_ref, woc_ref), (no_ref, noc_ref)):
            values = source[cut, :].astype(F32)
            target[cut, :] = (values - jnp.mean(values, axis=1, keepdims=True)).astype(BF16)

    midpad_ref[...] = jnp.zeros(midpad_ref.shape, F32)
    for i in range(mrows):
        midpad_ref[i * mcols : (i + 1) * mcols, :] = mid[i]
    terms_ref[rows + 2 * reach] = jnp.zeros((stride, hidden), BF16)

    for copy in copies:
        copy.wait()

    low3 = lax.broadcasted_iota(I32, (reach, 8, feature), 1) < 4
    above = jnp.where(low3, corner_dst[1].astype(F32), corner_dst[0].astype(F32)).astype(BF16)
    below = jnp.where(low3, corner_dst[3].astype(F32), corner_dst[2].astype(F32)).astype(BF16)
    for i in range(reach):
        for base, rows_of, corner in ((0, top, above), (reach, bottom, below)):
            begin = (base + i) * stride
            halo[begin : begin + cols, :] = rows_of[i]
            halo[begin + cols : begin + stride, :] = corner[i]
    fr = from_right[...].astype(F32)
    fl = from_left[...].astype(F32)
    beside = 2 * reach * stride
    middle = beside + half * 8
    halo[beside:middle, :] = jnp.where(low, fr, pltpu.roll(fl, 4, 1)).astype(BF16).reshape(half * 8, feature)
    halo[middle : middle + half * 8, :] = (
        jnp.where(low, pltpu.roll(fr, 4, 1), fl).astype(BF16).reshape(half * 8, feature)
    )

    @pl.loop(0, hidden // chunk)
    def _(c):
        far = (dot(halo[...], wsend_ref[:, lanes(c)]) * 0.5).astype(BF16)
        deep = reach * stride
        terms_ref[0:reach, :, lanes(c)] = far[0:deep].reshape(reach, stride, chunk)
        terms_ref[reach + rows : rows + 2 * reach, :, lanes(c)] = far[deep : 2 * deep].reshape(reach, stride, chunk)
        terms_ref[reach : reach + rows, cols:stride, lanes(c)] = far[2 * deep :].reshape(rows, 8, chunk)

    base = mrows * mcols
    midpad_ref[base : base + mcols, :] = mid_rows_dst[0].astype(F32)
    midpad_ref[base + mcols : base + 2 * mcols, :] = mid_rows_dst[1].astype(F32)
    for side, (tile, above, below, seat) in enumerate(((mid_left, 0, 2, mcols - 1), (mid_right, 1, 3, 0))):
        start = base + 2 * mcols + side * (mrows + 2) * mcols
        midpad_ref[start : start + mcols, :] = mid_corner[above].astype(F32)
        values = tile[...].astype(F32)
        for i in range(mrows):
            place = start + (i + 1) * mcols + seat
            midpad_ref[place : place + 1, :] = values[i : i + 1]
        finish = start + (mrows + 1) * mcols
        midpad_ref[finish : finish + mcols, :] = mid_corner[below].astype(F32)

    for load in (l_nsum, l_pool, l_prol):
        load.wait()

    def finish_pool(step, carry):
        pool_copy(step, other(step)).wait()
        return carry

    lax.fori_loop(1, total, finish_pool, 0)
    count = brows * bcols
    pooled_ref[0:count, :] = own_pool[...].astype(F32)
    for slot in range(1, total):
        pooled_ref[slot * count : (slot + 1) * count, :] = pools[slot].astype(F32)


def update_kernel(
    fanout, across, along, coarse_cols,
    x_ref, wrec_ref, e_ref, ns_ref, wsend_ref, wo_ref, no_ref, nsum_ref, pool_ref, prol_ref, ce_ref,
    zf_ref, zc_ref, zm_ref, xns_ref, terms_ref, pick_ref, pickm_ref, pickc_ref, me_ref, midpad_ref, pooled_ref,
    coarse_ref, ebias_ref, nbias_ref, egain_ref, eshift_ref, ngain_ref, nshift_ref,
    x_out, e_out, mid_out, mid_e_out, coarse_out, coarse_e_out,
    act, e_new, summed, fresh, x_new, mid_act, mid_flat, mid_new, mid_e_new, coarse_act, coarse_new, coarse_e_new,
    sems,
):
    places, feature = x_ref.shape
    hidden = wrec_ref.shape[1]
    chunk = 512
    mrows, mcols, _ = mid_new.shape
    mid_places = mrows * mcols
    coarse_places = coarse_ref.shape[0]
    cols = mcols * 4
    rows = places // cols
    stride = cols + 8
    window = pick_ref.shape[1]
    block = BLOCK * cols
    length = fanout * block
    pair = 2
    steps = rows // (BLOCK * pair)
    cuts = [slice(start, start + chunk) for start in range(0, hidden, chunk)]
    started = []

    def send(source, target):
        copy = pltpu.make_async_copy(source, target, sems.at[len(started)])
        copy.start()
        started.append(copy)

    def silu_half(values):
        small = values.astype(BF16)
        return small + small * jnp.tanh(small)

    def scaled(values, gain, shift):
        variance = jnp.mean(values * values, axis=-1, keepdims=True)
        return values * lax.rsqrt(variance + epsilon) * gain[...] + shift[...]

    def gather(step, sub):
        number = step * pair + sub
        here = slice(number * block, (number + 1) * block)
        begin = number * BLOCK * stride
        mine = pick_ref[number * length : (number + 1) * length, :]
        slot = step % act.shape[0]
        for cut in cuts:
            z = dot(mine, terms_ref[begin : begin + window, cut])
            z = z + zf_ref[:, here, cut].reshape(length, chunk).astype(F32)
            act[slot, sub * length : (sub + 1) * length, cut] = silu_half(z)

    def message(step):
        values = scaled(dot(act[step % act.shape[0]], wo_ref[...]), egain_ref, eshift_ref)
        for sub in range(pair):
            number = step * pair + sub
            here = slice(number * block, (number + 1) * block)
            part = values[sub * length : (sub + 1) * length].reshape(fanout, block, feature)
            new = e_ref[:, here, :].astype(F32) + part
            e_new[:, here, :] = new.astype(BF16)
            summed[here, :] = (jnp.sum(new, axis=0) * 0.5).astype(BF16)
        here = pl.ds(step * pair * block, pair * block)
        send(e_new.at[:, here, :], e_out.at[:, here, :])

    def node_hidden(own, incoming):
        return silu_half(own + dot(incoming, nsum_ref[...]))

    def node_final(nodes, inner):
        return nodes.astype(F32) + scaled(dot(inner, no_ref[...]), ngain_ref, nshift_ref)

    state = {}

    def coarse_start():
        me_x, me_y = lax.axis_index("dx"), lax.axis_index("dy")
        brows, bcols = mrows // 4, mcols // 4
        div, rem = lax.div, lax.rem
        row = lax.broadcasted_iota(I32, (coarse_places, 1), 0)
        line, column = div(row, coarse_cols), rem(row, coarse_cols)
        slot = rem(me_x * along + me_y + across * along - div(line, brows) * along - div(column, bcols), across * along)
        place = chosen(slot * (brows * bcols) + rem(line, brows) * bcols + rem(column, bcols), coarse_places)
        pooled = dot(place, pooled_ref[...].astype(BF16)).astype(BF16)
        pre = (coarse_ref[...].astype(F32) + dot(pooled, pool_ref[...])).astype(BF16)
        state["pre"] = pre
        state["term"] = (dot(pre, wsend_ref[...]) * 0.5).astype(BF16)
        state["receiver"] = (dot(pre, wrec_ref[...]) + ebias_ref[...]) * 0.5
        state["own"] = (dot(pre, ns_ref[...]) + nbias_ref[...]) * 0.5

    together = fanout if fanout * coarse_places <= length else 1

    def coarse_part(first):
        span = slice(first * coarse_places, (first + together) * coarse_places)
        for cut in cuts:
            z = dot(pickc_ref[span, :], state["term"][:, cut]) + zc_ref[span, cut].astype(F32)
            z = z.reshape(together, coarse_places, chunk) + state["receiver"][:, cut][None]
            coarse_act[:, cut] = silu_half(z.reshape(together * coarse_places, chunk))

    def coarse_gather():
        coarse_part(0)

    def coarse_message():
        incoming = jnp.zeros((coarse_places, feature), F32)
        for first in range(0, fanout, together):
            span = slice(first * coarse_places, (first + together) * coarse_places)
            if first:
                coarse_part(first)
            new = ce_ref[span, :].astype(F32) + scaled(dot(coarse_act[...], wo_ref[...]), egain_ref, eshift_ref)
            coarse_e_new[span, :] = new.astype(BF16)
            incoming = incoming + jnp.sum(new.reshape(together, coarse_places, feature), axis=0)
        send(coarse_e_new, coarse_e_out)
        state["incoming"] = (incoming * 0.5).astype(BF16)

    def coarse_node():
        inner = node_hidden(state["own"], state["incoming"])
        coarse = node_final(state["pre"], inner).astype(BF16)
        coarse_new[...] = coarse
        send(coarse_new, coarse_out)
        state["coarse"] = coarse

    def mid_start():
        me_x, me_y = lax.axis_index("dx"), lax.axis_index("dy")
        div, rem = lax.div, lax.rem
        row = lax.broadcasted_iota(I32, (midpad_ref.shape[0], 1), 0)
        beside = row - mid_places - 2 * mcols
        deep = (mrows + 2) * mcols
        seat = jnp.maximum(beside, 0)
        line = jnp.where(
            row < mid_places, div(row, mcols),
            jnp.where(row < mid_places + mcols, -1, jnp.where(beside < 0, mrows, div(rem(seat, deep), mcols) - 1)),
        )
        column = jnp.where(beside < 0, rem(row, mcols), jnp.where(beside < deep, -1, mcols))
        line = rem(me_x * mrows + line + across * mrows, across * mrows)
        column = rem(me_y * mcols + column + along * mcols, along * mcols)
        parent = dot(chosen(div(line, 4) * coarse_cols + div(column, 4), coarse_places), state["coarse"]).astype(BF16)
        padded = (midpad_ref[...] + dot(parent, prol_ref[...])).astype(BF16)
        pre = padded[:mid_places]
        state["pre"] = pre
        state["term"] = (dot(padded, wsend_ref[...]) * 0.5).astype(BF16)
        state["receiver"] = (dot(pre, wrec_ref[...]) + ebias_ref[...]) * 0.5
        state["own"] = (dot(pre, ns_ref[...]) + nbias_ref[...]) * 0.5

    def mid_gather():
        for cut in cuts:
            z = dot(pickm_ref[...], state["term"][:, cut]) + zm_ref[:, cut].astype(F32)
            z = z.reshape(fanout, mid_places, chunk) + state["receiver"][:, cut][None]
            mid_act[:, cut] = silu_half(z.reshape(fanout * mid_places, chunk))

    def mid_message():
        new = me_ref[...] + scaled(dot(mid_act[...], wo_ref[...]), egain_ref, eshift_ref)
        mid_flat[...] = new
        for i in range(fanout * mrows):
            mid_e_new[i] = mid_flat[i * mcols : (i + 1) * mcols, :].astype(BF16)
        send(mid_e_new, mid_e_out)
        state["incoming"] = (jnp.sum(new.reshape(fanout, mid_places, feature), axis=0) * 0.5).astype(BF16)

    def mid_node():
        inner = node_hidden(state["own"], state["incoming"])
        mid = node_final(state["pre"], inner).astype(BF16)
        values = mid.astype(F32)
        for i in range(mrows):
            mid_new[i] = values[i * mcols : (i + 1) * mcols].astype(BF16)
        send(mid_new, mid_out)
        state["lifted"] = dot(mid, prol_ref[...])

    pending = [
        coarse_start, coarse_gather, coarse_message, coarse_node, mid_start, mid_gather, mid_message, mid_node,
    ]

    def next_small():
        if pending:
            pending.pop(0)()

    next_small()
    for step in range(steps):
        for sub in range(pair):
            gather(step, sub)
        next_small()
        message(step)
    next_small()
    own = xns_ref[...].astype(F32)
    inner = node_hidden(own, summed[...])
    next_small()
    fresh[...] = node_final(x_ref[...], inner).astype(BF16)
    while pending:
        next_small()
    lifted = state["lifted"]
    for a in range(mrows):
        group = [
            jnp.broadcast_to(lifted[a * mcols + b : a * mcols + b + 1], (4, feature)) for b in range(mcols)
        ]
        lift = jnp.concatenate(group, axis=0)
        for i in range(4):
            here = slice((a * 4 + i) * cols, (a * 4 + i + 1) * cols)
            x_new[here, :] = (fresh[here, :].astype(F32) + lift).astype(BF16)
    send(x_new, x_out)
    for copy in started:
        copy.wait()


def per_device(
    fine_nodes, fine_edges, fine_links, mid_nodes, mid_edges, mid_links, coarse_nodes, coarse_edges,
    coarse_links, edge_self, edge_sender, edge_receiver, edge_bias, edge_output, edge_gain, edge_shift,
    node_self, node_summed, node_bias, node_output, node_gain, node_shift, prolongation, pooling,
):
    rows, cols, feature = fine_nodes.shape
    mrows, mcols, _ = mid_nodes.shape
    crows, ccols, _ = coarse_nodes.shape
    fanout = fine_edges.shape[0]
    across, along = lax.axis_size("dx"), lax.axis_size("dy")
    total = across * along
    places, mid_places, coarse_places = rows * cols, mrows * mcols, crows * ccols
    count = (mrows // 4) * (mcols // 4)
    stride = cols + 8
    hidden = edge_self.shape[2]
    window = round_up((BLOCK + 2 * FINE_REACH) * stride, 256)
    mid_total = round_up(3 * (mrows + 2) * mcols, 128)
    reach = FINE_REACH
    wide = BF16
    fuller = F32 if coarse_places * fanout <= places else BF16

    anywhere = pl.BlockSpec(memory_space=pl.ANY)
    vmem = pl.BlockSpec(memory_space=pltpu.VMEM)
    struct = jax.ShapeDtypeStruct
    fine_tile = pltpu.VMEM((rows, cols, feature), BF16)
    weight_in = pltpu.VMEM((feature, hidden), BF16)
    weight_out = pltpu.VMEM((hidden, feature), BF16)
    square = pltpu.VMEM((feature, feature), BF16)
    place = lambda *arrays: [pltpu.with_memory_space_constraint(array, pltpu.HBM) for array in arrays]
    front = pl.pallas_call(
        functools.partial(front_kernel, across, along),
        name="front",
        in_specs=[pl.BlockSpec(memory_space=pltpu.HBM)] * 19,
        out_shape=(
            fine_tile, weight_in, pltpu.VMEM((fanout, places, feature), BF16), weight_in, weight_in, weight_out, weight_out,
            weight_in, square, square, pltpu.VMEM((fanout * coarse_places, feature), BF16),
            pltpu.VMEM((fanout, places, hidden), wide), pltpu.VMEM((fanout * coarse_places, hidden), wide),
            pltpu.VMEM((fanout * mid_places, hidden), fuller), pltpu.VMEM((places, hidden), fuller),
            pltpu.VMEM((rows + 2 * reach + 1, stride, hidden), BF16), pltpu.VMEM((fanout * places, window), BF16),
            pltpu.VMEM((fanout * mid_places, mid_total), BF16), pltpu.VMEM((fanout * coarse_places, coarse_places), BF16),
            pltpu.VMEM((fanout * mid_places, feature), F32), pltpu.VMEM((mid_total, feature), F32),
            pltpu.VMEM((total * count, feature), F32),
        ),
        out_specs=[vmem] * 22,
        scratch_shapes=[
            pltpu.VMEM((mrows, mcols, feature), BF16),
            pltpu.VMEM((feature, hidden), BF16),
            pltpu.VMEM((fanout, cols, rows), I32),
            pltpu.VMEM((fanout, mcols, mrows), I32),
            pltpu.VMEM((fanout * crows, ccols), I32),
            pltpu.VMEM((1, hidden), F32),
            pltpu.VMEM((1, hidden), F32),
            pltpu.VMEM((fanout * mrows, mcols, feature), BF16),
            pltpu.VMEM((hidden, feature), BF16),
            pltpu.VMEM((hidden, feature), BF16),
            pltpu.VMEM((places, hidden), F32),
            pltpu.VMEM((2 * reach * stride + rows * 8, feature), BF16),
            pltpu.VMEM((rows // 2, 8, feature), BF16),
            pltpu.VMEM((rows // 2, 8, feature), BF16),
            pltpu.VMEM((4, reach, 8, feature), BF16),
            pltpu.VMEM((reach, cols, feature), BF16),
            pltpu.VMEM((reach, cols, feature), BF16),
            pltpu.VMEM((rows // 2, 8, feature), BF16),
            pltpu.VMEM((rows // 2, 8, feature), BF16),
            pltpu.VMEM((4, reach, 8, feature), BF16),
            pltpu.VMEM((2, mrows, feature), BF16),
            pltpu.VMEM((2, mcols, feature), BF16),
            pltpu.VMEM((mrows, feature), BF16),
            pltpu.VMEM((mrows, feature), BF16),
            pltpu.VMEM((4, mcols, feature), BF16),
            pltpu.VMEM((count, feature), BF16),
            pltpu.VMEM((total, count, feature), BF16),
            pltpu.SemaphoreType.DMA((20,)),
            pltpu.SemaphoreType.DMA((16,)),
            pltpu.SemaphoreType.DMA((16,)),
            pltpu.SemaphoreType.DMA((total,)),
            pltpu.SemaphoreType.DMA((total,)),
        ],
        compiler_params=pltpu.CompilerParams(
            collective_id=0, has_side_effects=True, vmem_limit_bytes=FRONT_MIB * 1024 * 1024
        ),
    )(*place(
        fine_nodes, mid_nodes, edge_receiver[0], edge_self[0], fine_edges.reshape(fanout, places, feature),
        node_self[0], edge_sender[0], jnp.swapaxes(fine_links, 1, 2), jnp.swapaxes(mid_links, 1, 2),
        coarse_links.reshape(fanout * crows, ccols), edge_bias, node_bias,
        coarse_edges.reshape(fanout * coarse_places, feature), mid_edges.reshape(fanout * mrows, mcols, feature),
        edge_output[0], node_output[0], node_summed[0], pooling[0], prolongation[0],
    ))
    front = list(front)
    front[0] = front[0].reshape(places, feature)
    front[15] = front[15].reshape(-1, hidden)
    front = [pltpu.with_memory_space_constraint(array, pltpu.VMEM) for array in front]
    length = fanout * BLOCK * cols
    coarse_rows = fanout * coarse_places if fanout * coarse_places <= length else coarse_places
    fine_out, fine_e, mid_out, mid_e, coarse_out, coarse_e = pl.pallas_call(
        functools.partial(update_kernel, fanout, across, along, ccols),
        name="update",
        in_specs=[vmem] * 29,
        out_shape=(
            struct((places, feature), BF16),
            struct((fanout, places, feature), BF16),
            struct((mrows, mcols, feature), BF16),
            struct((fanout * mrows, mcols, feature), BF16),
            struct((coarse_places, feature), BF16),
            struct((fanout * coarse_places, feature), BF16),
        ),
        out_specs=[anywhere] * 6,
        scratch_shapes=[
            pltpu.VMEM((2 if fanout * coarse_places <= length else 1, 2 * length, hidden), BF16),
            pltpu.VMEM((fanout, places, feature), BF16),
            pltpu.VMEM((places, feature), BF16),
            pltpu.VMEM((places, feature), BF16),
            pltpu.VMEM((places, feature), BF16),
            pltpu.VMEM((fanout * mid_places, hidden), BF16),
            pltpu.VMEM((fanout * mid_places, feature), F32),
            pltpu.VMEM((mrows, mcols, feature), BF16),
            pltpu.VMEM((fanout * mrows, mcols, feature), BF16),
            pltpu.VMEM((coarse_rows, hidden), BF16),
            pltpu.VMEM((coarse_places, feature), BF16),
            pltpu.VMEM((fanout * coarse_places, feature), BF16),
            pltpu.SemaphoreType.DMA((16,)),
        ],
        compiler_params=pltpu.CompilerParams(vmem_limit_bytes=(18 if fanout * coarse_places <= length else 20) * 1024 * 1024),
    )(
        *front, coarse_nodes.reshape(coarse_places, feature), edge_bias, node_bias, edge_gain, edge_shift,
        node_gain, node_shift,
    )
    return (
        fine_out.reshape(fine_nodes.shape),
        fine_e.reshape(fine_edges.shape),
        mid_out.reshape(mid_nodes.shape),
        mid_e.reshape(mid_edges.shape),
        coarse_out.reshape(coarse_nodes.shape),
        coarse_e.reshape(coarse_edges.shape),
    )


FRONT_MIB = 11


def solution(mesh):
    tile = P("dx", "dy", None)
    edge_tile = P(None, "dx", "dy", None)
    link_tile = P(None, "dx", "dy")
    return jax.shard_map(
        per_device,
        mesh=mesh,
        in_specs=(tile, edge_tile, link_tile) * 2 + (P(),) * 18,
        out_specs=(tile, edge_tile, tile, edge_tile, P(), P()),
        check_vma=False,
    )
```

```python
import functools

import jax
import jax.numpy as jnp
from jax import lax
from jax.experimental import pallas as pl
from jax.experimental.pallas import tpu as pltpu
from jax.sharding import PartitionSpec as P

FINE_REACH = 3
MID_REACH = 1
BLOCK = 4
epsilon = 1e-05
F32 = jnp.float32
BF16 = jnp.bfloat16
I32 = jnp.int32


def round_up(value, unit):
    return -(-value // unit) * unit


def dot(a, b):
    return jnp.dot(a, b, preferred_element_type=F32)


def spread(values, length):
    lines, width = values.shape
    row = lax.broadcasted_iota(I32, (length, lines), 0)
    line = lax.broadcasted_iota(I32, (length, lines), 1) * width
    owner = jnp.where((row >= line) & (row < line + width), 1.0, 0.0).astype(BF16)
    rows = dot(owner, values.astype(BF16))
    row = lax.broadcasted_iota(I32, (length, width), 0)
    lane = lax.broadcasted_iota(I32, (length, width), 1)
    return jnp.sum(jnp.where(lax.rem(row, width) == lane, rows, 0.0), axis=1, keepdims=True)


def chosen(column, width):
    lane = lax.broadcasted_iota(I32, (column.shape[0], width), 1).astype(column.dtype)
    return jnp.where(column == lane, 1.0, 0.0).astype(BF16)


def front_kernel(
    across, along,
    x_hbm, mid_hbm, wrec_hbm, ws_hbm, e_hbm, ns_hbm, wsend_hbm, links_hbm, mid_links_hbm, coarse_links_hbm,
    ebias_hbm, nbias_hbm, ce_hbm, me_hbm, wo_hbm, no_hbm, nsum_hbm, pool_hbm, prol_hbm,
    x_ref, wrec_ref, e_ref, ns_ref, wsend_ref, woc_ref, noc_ref, nsum_ref, pool_ref, prol_ref, ce_ref,
    zf_ref, zc_ref, zm_ref, xns_ref, terms_ref, pick_ref, pickm_ref, pickc_ref, me_ref, midpad_ref, pooled_ref,
    mid_ref, ws_ref, links_ref, mid_links_ref, coarse_links_ref, ebias_ref, nbias_ref, mid_e_ref, wo_ref, no_ref,
    receivers, halo,
    to_left, to_right, corner_src, top, bottom, from_left, from_right, corner_dst,
    mid_src, mid_rows_dst, mid_left, mid_right, mid_corner, pools,
    load_sem, near_send, near_recv, pool_send, pool_recv, far_send, far_recv,
):
    rows, cols, feature = x_ref.shape
    mrows, mcols, _ = mid_ref.shape
    fanout, places, hidden = zf_ref.shape
    half = rows // 2
    reach = FINE_REACH
    stride = cols + 8
    me_x = lax.axis_index("dx")
    me_y = lax.axis_index("dy")
    up = lax.rem(me_x + across - 1, across)
    down = lax.rem(me_x + 1, across)
    left = lax.rem(me_y + along - 1, along)
    right = lax.rem(me_y + 1, along)

    def beside_y(step):
        return me_x, lax.rem(me_y + step, along)

    def beside_x(step):
        return lax.rem(me_x + step, across), me_y

    group = fanout // 2
    loads = (
        (mid_hbm, mid_ref), (x_hbm, x_ref), (wrec_hbm, wrec_ref), (ebias_hbm, ebias_ref), (ws_hbm, ws_ref),
        (e_hbm.at[pl.ds(0, group)], e_ref.at[pl.ds(0, group)]),
        (e_hbm.at[pl.ds(group, group)], e_ref.at[pl.ds(group, group)]),
        (ns_hbm, ns_ref), (nbias_hbm, nbias_ref), (wsend_hbm, wsend_ref),
        (links_hbm, links_ref), (mid_links_hbm, mid_links_ref), (coarse_links_hbm, coarse_links_ref),
        (ce_hbm, ce_ref), (me_hbm, mid_e_ref), (wo_hbm, wo_ref), (no_hbm, no_ref), (nsum_hbm, nsum_ref),
        (pool_hbm, pool_ref), (prol_hbm, prol_ref),
    )
    loads = [pltpu.make_async_copy(source, target, load_sem.at[n]) for n, (source, target) in enumerate(loads)]
    (l_mid, l_x, l_wrec, l_ebias, l_ws, l_e0, l_e1, l_ns, l_nbias, l_wsend, l_links, l_mlinks, l_clinks,
     l_ce, l_me, l_wo, l_no, l_nsum, l_pool, l_prol) = loads
    for load in loads:
        load.start()

    barrier = pltpu.get_barrier_semaphore()

    def greet(device):
        pl.semaphore_signal(barrier, inc=1, device_id=device, device_id_type=pl.DeviceIdType.MESH)

    for step in range(1, along):
        greet(beside_y(step))
    for step in range(1, across):
        greet(beside_x(step))
    for device in ((down, right), (down, left), (up, right), (up, left)):
        greet(device)

    l_mid.wait()
    mid = mid_ref[...].astype(F32)
    brows, bcols = mrows // 4, mcols // 4
    means = []
    for i in range(brows):
        strip = jnp.sum(mid[4 * i : 4 * i + 4], axis=0)
        for j in range(bcols):
            means.append(jnp.sum(strip[4 * j : 4 * j + 4], axis=0, keepdims=True) * (1.0 / 16.0))
    pools[0, 0] = jnp.concatenate(means, axis=0).astype(BF16)
    mid_src[0] = jnp.concatenate([mid[i, mcols - 1 : mcols] for i in range(mrows)], axis=0).astype(BF16)
    mid_src[1] = jnp.concatenate([mid[i, 0:1] for i in range(mrows)], axis=0).astype(BF16)

    l_x.wait()
    low = lax.broadcasted_iota(I32, (half, 8, feature), 1) < 4
    first_a = x_ref[0:half, 0:8].astype(F32)
    first_b = x_ref[half:rows, 0:8].astype(F32)
    to_left[...] = jnp.where(low, first_a, pltpu.roll(first_b, 4, 1)).astype(BF16)
    last_a = x_ref[0:half, cols - 8 : cols].astype(F32)
    last_b = x_ref[half:rows, cols - 8 : cols].astype(F32)
    to_right[...] = jnp.where(low, pltpu.roll(last_a, 4, 1), last_b).astype(BF16)
    corner_src[0] = x_ref[rows - reach : rows, cols - 8 : cols]
    corner_src[1] = x_ref[rows - reach : rows, 0:8]
    corner_src[2] = x_ref[0:reach, cols - 8 : cols]
    corner_src[3] = x_ref[0:reach, 0:8]

    chunk = 512
    lanes = lambda c: slice(c * chunk, (c + 1) * chunk)
    chunks = range(hidden // chunk)
    light = []

    def beside(number):
        for _ in range(min(number, len(light))):
            light.pop(0)()

    l_wrec.wait()
    l_ebias.wait()

    for c in chunks:
        flat = x_ref[...].reshape(places, feature)
        receivers[:, lanes(c)] = (dot(flat, wrec_ref[:, lanes(c)]) + ebias_ref[:, lanes(c)]) * 0.5

    def own_edges(first, columns):
        for c in columns:
            beside(3)
            edges = e_ref[first : first + group].reshape(group * places, feature)
            z = dot(edges, ws_ref[:, lanes(c)]) * 0.5
            z = z.reshape(group, places, chunk) + receivers[:, lanes(c)][None]
            zf_ref[first : first + group, :, lanes(c)] = z.astype(zf_ref.dtype)

    l_ws.wait()
    l_e0.wait()
    own_edges(0, chunks[:1])

    pl.semaphore_wait(barrier, along + across + 2)

    line_copies = []
    for step in range(1, along):
        copy = pltpu.make_async_remote_copy(
            src_ref=pools.at[0, 0], dst_ref=pools.at[0, step], send_sem=pool_send.at[step],
            recv_sem=pool_recv.at[step], device_id=beside_y(step), device_id_type=pl.DeviceIdType.MESH,
        )
        copy.start()
        line_copies.append(copy)

    plan = (
        (to_right, from_left, (me_x, right)),
        (to_left, from_right, (me_x, left)),
        (x_ref.at[pl.ds(rows - reach, reach)], top, (down, me_y)),
        (x_ref.at[pl.ds(0, reach)], bottom, (up, me_y)),
        (corner_src.at[0], corner_dst.at[0], (down, right)),
        (corner_src.at[1], corner_dst.at[1], (down, left)),
        (corner_src.at[2], corner_dst.at[2], (up, right)),
        (corner_src.at[3], corner_dst.at[3], (up, left)),
        (mid_src.at[0], mid_left, (me_x, right)),
        (mid_src.at[1], mid_right, (me_x, left)),
        (mid_ref.at[mrows - 1], mid_rows_dst.at[0], (down, me_y)),
        (mid_ref.at[0], mid_rows_dst.at[1], (up, me_y)),
        (mid_ref.at[mrows - 1], mid_corner.at[0], (down, right)),
        (mid_ref.at[mrows - 1], mid_corner.at[1], (down, left)),
        (mid_ref.at[0], mid_corner.at[2], (up, right)),
        (mid_ref.at[0], mid_corner.at[3], (up, left)),
    )
    copies = []
    far_copies = []
    for number, (source, target, device) in enumerate(plan):
        copy = pltpu.make_async_remote_copy(
            src_ref=source, dst_ref=target, send_sem=near_send.at[number],
            recv_sem=near_recv.at[number], device_id=device, device_id_type=pl.DeviceIdType.MESH,
        )
        copy.start()
        copies.append(copy)


    own_edges(0, chunks[1:])

    l_e1.wait()
    l_ns.wait()
    l_nbias.wait()
    l_wsend.wait()
    l_ce.wait()
    l_me.wait()
    rem, div = lax.rem, lax.div
    l_links.wait()
    links = links_ref[...]
    span = 2 * FINE_REACH + 1
    column = lax.broadcasted_iota(I32, links.shape, 1) + rem(links, span) + (stride - FINE_REACH)
    line = rem(lax.broadcasted_iota(I32, links.shape, 2), BLOCK) + div(links, span)
    index = line * stride + rem(column, stride)
    window = pick_ref.shape[1]
    lane = lax.broadcasted_iota(I32, (cols, window), 1)

    def pick_block(s):
        for k in range(fanout):
            for i in range(BLOCK):
                x = s * BLOCK + i
                hit = jnp.where(index[k, :, x : x + 1] == lane, 1.0, 0.0).astype(BF16)
                begin = ((s * fanout + k) * BLOCK + i) * cols
                pick_ref[begin : begin + cols, :] = hit

    light += [functools.partial(pick_block, s) for s in range(rows // BLOCK)]
    l_wo.wait()
    l_no.wait()

    def centre_block(source, target, start):
        values = source[start : start + 256, :].astype(F32)
        target[start : start + 256, :] = (values - jnp.mean(values, axis=1, keepdims=True)).astype(BF16)

    for start in range(0, hidden, 256):
        light.append(functools.partial(centre_block, wo_ref, woc_ref, start))
        light.append(functools.partial(centre_block, no_ref, noc_ref, start))

    own_edges(group, chunks)

    for copy in line_copies:
        copy.wait()
    for step in range(1, across):
        copy = pltpu.make_async_remote_copy(
            src_ref=pools.at[0], dst_ref=pools.at[step], send_sem=far_send.at[step],
            recv_sem=far_recv.at[step], device_id=beside_x(step), device_id_type=pl.DeviceIdType.MESH,
        )
        copy.start()
        far_copies.append(copy)


    for c in chunks:
        beside(2)
        flat = x_ref[...].reshape(places, feature)
        own = (dot(flat, ns_ref[:, lanes(c)]) + nbias_ref[:, lanes(c)]) * 0.5
        xns_ref[:, lanes(c)] = own.astype(xns_ref.dtype)
        own = (dot(flat, wsend_ref[:, lanes(c)]) * 0.5).astype(BF16)
        terms_ref[reach : reach + rows, 0:cols, lanes(c)] = own.reshape(rows, cols, chunk)

    for i in range(fanout * mrows):
        me_ref[i * mcols : (i + 1) * mcols, :] = mid_e_ref[i].astype(F32)

    for c in chunks:
        beside(2)
        zc_ref[:, lanes(c)] = (dot(ce_ref[...], ws_ref[:, lanes(c)]) * 0.5).astype(zc_ref.dtype)
        zm_ref[:, lanes(c)] = (dot(me_ref[...].astype(BF16), ws_ref[:, lanes(c)]) * 0.5).astype(zm_ref.dtype)

    beside(len(light))
    mid_places = mrows * mcols
    l_mlinks.wait()
    l_clinks.wait()
    links = mid_links_ref[...]
    line = lax.broadcasted_iota(I32, links.shape, 2) + div(links, 3) - 1
    column = lax.broadcasted_iota(I32, links.shape, 1) + rem(links, 3) - 1
    centre = jnp.where(
        line < 0, mid_places + column,
        jnp.where(line >= mrows, mid_places + mcols + column, line * mcols + column),
    )
    side = mid_places + 2 * mcols + (line + 1) * mcols
    index = jnp.where(column < 0, side + mcols - 1, jnp.where(column >= mcols, side + (mrows + 2) * mcols, centre))
    mid_total = pickm_ref.shape[1]
    lane = lax.broadcasted_iota(I32, (mcols, mid_total), 1)
    for k in range(fanout):
        for x in range(0, mrows, 4):
            pieces = [jnp.where(index[k, :, x + i : x + i + 1] == lane, 1.0, 0.0) for i in range(4)]
            begin = (k * mrows + x) * mcols
            pickm_ref[begin : begin + 4 * mcols, :] = jnp.concatenate(pieces, axis=0).astype(BF16)
    links = coarse_links_ref[...].astype(F32)
    count = pickc_ref.shape[0]
    pickc_ref[...] = chosen(spread(links, count), pickc_ref.shape[1])

    midpad_ref[...] = jnp.zeros(midpad_ref.shape, F32)
    for i in range(mrows):
        midpad_ref[i * mcols : (i + 1) * mcols, :] = mid[i]
    terms_ref[rows + 2 * reach] = jnp.zeros((stride, hidden), BF16)

    for copy in copies:
        copy.wait()

    low3 = lax.broadcasted_iota(I32, (reach, 8, feature), 1) < 4
    above = jnp.where(low3, corner_dst[1].astype(F32), corner_dst[0].astype(F32)).astype(BF16)
    below = jnp.where(low3, corner_dst[3].astype(F32), corner_dst[2].astype(F32)).astype(BF16)
    for i in range(reach):
        for base, rows_of, corner in ((0, top, above), (reach, bottom, below)):
            begin = (base + i) * stride
            halo[begin : begin + cols, :] = rows_of[i]
            halo[begin + cols : begin + stride, :] = corner[i]
    fr = from_right[...].astype(F32)
    fl = from_left[...].astype(F32)
    beside = 2 * reach * stride
    middle = beside + half * 8
    halo[beside:middle, :] = jnp.where(low, fr, pltpu.roll(fl, 4, 1)).astype(BF16).reshape(half * 8, feature)
    halo[middle : middle + half * 8, :] = (
        jnp.where(low, pltpu.roll(fr, 4, 1), fl).astype(BF16).reshape(half * 8, feature)
    )

    for c in chunks:
        far = (dot(halo[...], wsend_ref[:, lanes(c)]) * 0.5).astype(BF16)
        deep = reach * stride
        terms_ref[0:reach, :, lanes(c)] = far[0:deep].reshape(reach, stride, chunk)
        terms_ref[reach + rows : rows + 2 * reach, :, lanes(c)] = far[deep : 2 * deep].reshape(reach, stride, chunk)
        terms_ref[reach : reach + rows, cols:stride, lanes(c)] = far[2 * deep :].reshape(rows, 8, chunk)

    base = mrows * mcols
    midpad_ref[base : base + mcols, :] = mid_rows_dst[0].astype(F32)
    midpad_ref[base + mcols : base + 2 * mcols, :] = mid_rows_dst[1].astype(F32)
    for side, (tile, above, below, seat) in enumerate(((mid_left, 0, 2, mcols - 1), (mid_right, 1, 3, 0))):
        start = base + 2 * mcols + side * (mrows + 2) * mcols
        midpad_ref[start : start + mcols, :] = mid_corner[above].astype(F32)
        values = tile[...].astype(F32)
        for i in range(mrows):
            place = start + (i + 1) * mcols + seat
            midpad_ref[place : place + 1, :] = values[i : i + 1]
        finish = start + (mrows + 1) * mcols
        midpad_ref[finish : finish + mcols, :] = mid_corner[below].astype(F32)

    for load in (l_nsum, l_pool, l_prol):
        load.wait()

    for copy in far_copies:
        copy.wait()
    count = brows * bcols
    for step in range(across):
        for slot in range(along):
            begin = (step * along + slot) * count
            pooled_ref[begin : begin + count, :] = pools[step, slot].astype(F32)


def update_kernel(
    fanout, across, along, coarse_cols,
    x_ref, wrec_ref, e_ref, ns_ref, wsend_ref, wo_ref, no_ref, nsum_ref, pool_ref, prol_ref, ce_ref,
    zf_ref, zc_ref, zm_ref, xns_ref, terms_ref, pick_ref, pickm_ref, pickc_ref, me_ref, midpad_ref, pooled_ref,
    coarse_ref, ebias_ref, nbias_ref, egain_ref, eshift_ref, ngain_ref, nshift_ref,
    x_out, e_out, mid_out, mid_e_out, coarse_out, coarse_e_out,
    act, e_new, summed, fresh, x_new, mid_act, mid_flat, mid_new, mid_e_new, coarse_act, coarse_new, coarse_e_new,
    sems,
):
    places, feature = x_ref.shape
    hidden = wrec_ref.shape[1]
    chunk = 512
    mrows, mcols, _ = mid_new.shape
    mid_places = mrows * mcols
    coarse_places = coarse_ref.shape[0]
    cols = mcols * 4
    rows = places // cols
    stride = cols + 8
    window = pick_ref.shape[1]
    block = BLOCK * cols
    length = fanout * block
    pair = 2
    steps = rows // (BLOCK * pair)
    cuts = [slice(start, start + chunk) for start in range(0, hidden, chunk)]
    started = []

    def send(source, target):
        copy = pltpu.make_async_copy(source, target, sems.at[len(started)])
        copy.start()
        started.append(copy)

    def silu_half(values):
        small = values.astype(BF16)
        return small + small * jnp.tanh(small)

    def scaled(values, gain, shift):
        variance = jnp.mean(values * values, axis=-1, keepdims=True)
        return values * lax.rsqrt(variance + epsilon) * gain[...] + shift[...]

    def gather(step, sub):
        number = step * pair + sub
        here = slice(number * block, (number + 1) * block)
        begin = number * BLOCK * stride
        mine = pick_ref[number * length : (number + 1) * length, :]
        slot = step % act.shape[0]
        for cut in cuts:
            z = dot(mine, terms_ref[begin : begin + window, cut])
            z = z + zf_ref[:, here, cut].reshape(length, chunk).astype(F32)
            act[slot, sub * length : (sub + 1) * length, cut] = silu_half(z)

    def message(step):
        values = scaled(dot(act[step % act.shape[0]], wo_ref[...]), egain_ref, eshift_ref)
        for sub in range(pair):
            number = step * pair + sub
            here = slice(number * block, (number + 1) * block)
            part = values[sub * length : (sub + 1) * length].reshape(fanout, block, feature)
            new = e_ref[:, here, :].astype(F32) + part
            e_new[:, here, :] = new.astype(BF16)
            summed[here, :] = (jnp.sum(new, axis=0) * 0.5).astype(BF16)
        here = pl.ds(step * pair * block, pair * block)
        send(e_new.at[:, here, :], e_out.at[:, here, :])

    def node_hidden(own, incoming):
        return silu_half(own + dot(incoming, nsum_ref[...]))

    def node_final(nodes, inner):
        return nodes.astype(F32) + scaled(dot(inner, no_ref[...]), ngain_ref, nshift_ref)

    state = {}

    def coarse_start():
        me_x, me_y = lax.axis_index("dx"), lax.axis_index("dy")
        brows, bcols = mrows // 4, mcols // 4
        div, rem = lax.div, lax.rem
        row = lax.broadcasted_iota(I32, (coarse_places, 1), 0)
        line, column = div(row, coarse_cols), rem(row, coarse_cols)
        slot = rem(me_x + across - div(line, brows), across) * along + rem(me_y + along - div(column, bcols), along)
        place = chosen(slot * (brows * bcols) + rem(line, brows) * bcols + rem(column, bcols), coarse_places)
        pooled = dot(place, pooled_ref[...].astype(BF16)).astype(BF16)
        pre = (coarse_ref[...].astype(F32) + dot(pooled, pool_ref[...])).astype(BF16)
        state["pre"] = pre
        state["term"] = (dot(pre, wsend_ref[...]) * 0.5).astype(BF16)
        state["receiver"] = (dot(pre, wrec_ref[...]) + ebias_ref[...]) * 0.5
        state["own"] = (dot(pre, ns_ref[...]) + nbias_ref[...]) * 0.5

    together = fanout if fanout * coarse_places <= length else 1

    def coarse_part(first):
        span = slice(first * coarse_places, (first + together) * coarse_places)
        for cut in cuts:
            z = dot(pickc_ref[span, :], state["term"][:, cut]) + zc_ref[span, cut].astype(F32)
            z = z.reshape(together, coarse_places, chunk) + state["receiver"][:, cut][None]
            coarse_act[:, cut] = silu_half(z.reshape(together * coarse_places, chunk))

    def coarse_gather():
        coarse_part(0)

    def coarse_message():
        incoming = jnp.zeros((coarse_places, feature), F32)
        for first in range(0, fanout, together):
            span = slice(first * coarse_places, (first + together) * coarse_places)
            if first:
                coarse_part(first)
            new = ce_ref[span, :].astype(F32) + scaled(dot(coarse_act[...], wo_ref[...]), egain_ref, eshift_ref)
            coarse_e_new[span, :] = new.astype(BF16)
            incoming = incoming + jnp.sum(new.reshape(together, coarse_places, feature), axis=0)
        send(coarse_e_new, coarse_e_out)
        state["incoming"] = (incoming * 0.5).astype(BF16)

    def coarse_node():
        inner = node_hidden(state["own"], state["incoming"])
        coarse = node_final(state["pre"], inner).astype(BF16)
        coarse_new[...] = coarse
        send(coarse_new, coarse_out)
        state["coarse"] = coarse

    def mid_start():
        me_x, me_y = lax.axis_index("dx"), lax.axis_index("dy")
        div, rem = lax.div, lax.rem
        row = lax.broadcasted_iota(I32, (midpad_ref.shape[0], 1), 0)
        beside = row - mid_places - 2 * mcols
        deep = (mrows + 2) * mcols
        seat = jnp.maximum(beside, 0)
        line = jnp.where(
            row < mid_places, div(row, mcols),
            jnp.where(row < mid_places + mcols, -1, jnp.where(beside < 0, mrows, div(rem(seat, deep), mcols) - 1)),
        )
        column = jnp.where(beside < 0, rem(row, mcols), jnp.where(beside < deep, -1, mcols))
        line = rem(me_x * mrows + line + across * mrows, across * mrows)
        column = rem(me_y * mcols + column + along * mcols, along * mcols)
        parent = dot(chosen(div(line, 4) * coarse_cols + div(column, 4), coarse_places), state["coarse"]).astype(BF16)
        padded = (midpad_ref[...] + dot(parent, prol_ref[...])).astype(BF16)
        pre = padded[:mid_places]
        state["pre"] = pre
        state["term"] = (dot(padded, wsend_ref[...]) * 0.5).astype(BF16)
        state["receiver"] = (dot(pre, wrec_ref[...]) + ebias_ref[...]) * 0.5
        state["own"] = (dot(pre, ns_ref[...]) + nbias_ref[...]) * 0.5

    def mid_gather():
        for cut in cuts:
            z = dot(pickm_ref[...], state["term"][:, cut]) + zm_ref[:, cut].astype(F32)
            z = z.reshape(fanout, mid_places, chunk) + state["receiver"][:, cut][None]
            mid_act[:, cut] = silu_half(z.reshape(fanout * mid_places, chunk))

    def mid_message():
        new = me_ref[...] + scaled(dot(mid_act[...], wo_ref[...]), egain_ref, eshift_ref)
        mid_flat[...] = new
        for i in range(fanout * mrows):
            mid_e_new[i] = mid_flat[i * mcols : (i + 1) * mcols, :].astype(BF16)
        send(mid_e_new, mid_e_out)
        state["incoming"] = (jnp.sum(new.reshape(fanout, mid_places, feature), axis=0) * 0.5).astype(BF16)

    def mid_node():
        inner = node_hidden(state["own"], state["incoming"])
        mid = node_final(state["pre"], inner).astype(BF16)
        values = mid.astype(F32)
        for i in range(mrows):
            mid_new[i] = values[i * mcols : (i + 1) * mcols].astype(BF16)
        send(mid_new, mid_out)
        state["lifted"] = dot(mid, prol_ref[...])

    pending = [
        coarse_start, coarse_gather, coarse_message, coarse_node, mid_start, mid_gather, mid_message, mid_node,
    ]

    def next_small():
        if pending:
            pending.pop(0)()

    next_small()
    for step in range(steps):
        for sub in range(pair):
            gather(step, sub)
        next_small()
        message(step)
    next_small()
    own = xns_ref[...].astype(F32)
    inner = node_hidden(own, summed[...])
    next_small()
    fresh[...] = node_final(x_ref[...], inner).astype(BF16)
    while pending:
        next_small()
    lifted = state["lifted"]
    for a in range(mrows):
        group = [
            jnp.broadcast_to(lifted[a * mcols + b : a * mcols + b + 1], (4, feature)) for b in range(mcols)
        ]
        lift = jnp.concatenate(group, axis=0)
        for i in range(4):
            here = slice((a * 4 + i) * cols, (a * 4 + i + 1) * cols)
            x_new[here, :] = (fresh[here, :].astype(F32) + lift).astype(BF16)
    send(x_new, x_out)
    for copy in started:
        copy.wait()


def per_device(
    fine_nodes, fine_edges, fine_links, mid_nodes, mid_edges, mid_links, coarse_nodes, coarse_edges,
    coarse_links, edge_self, edge_sender, edge_receiver, edge_bias, edge_output, edge_gain, edge_shift,
    node_self, node_summed, node_bias, node_output, node_gain, node_shift, prolongation, pooling,
):
    rows, cols, feature = fine_nodes.shape
    mrows, mcols, _ = mid_nodes.shape
    crows, ccols, _ = coarse_nodes.shape
    fanout = fine_edges.shape[0]
    across, along = lax.axis_size("dx"), lax.axis_size("dy")
    total = across * along
    places, mid_places, coarse_places = rows * cols, mrows * mcols, crows * ccols
    count = (mrows // 4) * (mcols // 4)
    stride = cols + 8
    hidden = edge_self.shape[2]
    window = round_up((BLOCK + 2 * FINE_REACH) * stride, 256)
    mid_total = round_up(3 * (mrows + 2) * mcols, 128)
    reach = FINE_REACH
    wide = BF16
    fuller = F32 if coarse_places * fanout <= places else BF16

    anywhere = pl.BlockSpec(memory_space=pl.ANY)
    vmem = pl.BlockSpec(memory_space=pltpu.VMEM)
    struct = jax.ShapeDtypeStruct
    fine_tile = pltpu.VMEM((rows, cols, feature), BF16)
    weight_in = pltpu.VMEM((feature, hidden), BF16)
    weight_out = pltpu.VMEM((hidden, feature), BF16)
    square = pltpu.VMEM((feature, feature), BF16)
    place = lambda *arrays: [pltpu.with_memory_space_constraint(array, pltpu.HBM) for array in arrays]
    front = pl.pallas_call(
        functools.partial(front_kernel, across, along),
        name="front",
        in_specs=[pl.BlockSpec(memory_space=pltpu.HBM)] * 19,
        out_shape=(
            fine_tile, weight_in, pltpu.VMEM((fanout, places, feature), BF16), weight_in, weight_in, weight_out, weight_out,
            weight_in, square, square, pltpu.VMEM((fanout * coarse_places, feature), BF16),
            pltpu.VMEM((fanout, places, hidden), wide), pltpu.VMEM((fanout * coarse_places, hidden), wide),
            pltpu.VMEM((fanout * mid_places, hidden), fuller), pltpu.VMEM((places, hidden), fuller),
            pltpu.VMEM((rows + 2 * reach + 1, stride, hidden), BF16), pltpu.VMEM((fanout * places, window), BF16),
            pltpu.VMEM((fanout * mid_places, mid_total), BF16), pltpu.VMEM((fanout * coarse_places, coarse_places), BF16),
            pltpu.VMEM((fanout * mid_places, feature), F32), pltpu.VMEM((mid_total, feature), F32),
            pltpu.VMEM((total * count, feature), F32),
        ),
        out_specs=[vmem] * 22,
        scratch_shapes=[
            pltpu.VMEM((mrows, mcols, feature), BF16),
            pltpu.VMEM((feature, hidden), BF16),
            pltpu.VMEM((fanout, cols, rows), I32),
            pltpu.VMEM((fanout, mcols, mrows), I32),
            pltpu.VMEM((fanout * crows, ccols), I32),
            pltpu.VMEM((1, hidden), F32),
            pltpu.VMEM((1, hidden), F32),
            pltpu.VMEM((fanout * mrows, mcols, feature), BF16),
            pltpu.VMEM((hidden, feature), BF16),
            pltpu.VMEM((hidden, feature), BF16),
            pltpu.VMEM((places, hidden), F32),
            pltpu.VMEM((2 * reach * stride + rows * 8, feature), BF16),
            pltpu.VMEM((rows // 2, 8, feature), BF16),
            pltpu.VMEM((rows // 2, 8, feature), BF16),
            pltpu.VMEM((4, reach, 8, feature), BF16),
            pltpu.VMEM((reach, cols, feature), BF16),
            pltpu.VMEM((reach, cols, feature), BF16),
            pltpu.VMEM((rows // 2, 8, feature), BF16),
            pltpu.VMEM((rows // 2, 8, feature), BF16),
            pltpu.VMEM((4, reach, 8, feature), BF16),
            pltpu.VMEM((2, mrows, feature), BF16),
            pltpu.VMEM((2, mcols, feature), BF16),
            pltpu.VMEM((mrows, feature), BF16),
            pltpu.VMEM((mrows, feature), BF16),
            pltpu.VMEM((4, mcols, feature), BF16),
            pltpu.VMEM((across, along, count, feature), BF16),
            pltpu.SemaphoreType.DMA((20,)),
            pltpu.SemaphoreType.DMA((16,)),
            pltpu.SemaphoreType.DMA((16,)),
            pltpu.SemaphoreType.DMA((along,)),
            pltpu.SemaphoreType.DMA((along,)),
            pltpu.SemaphoreType.DMA((across,)),
            pltpu.SemaphoreType.DMA((across,)),
        ],
        compiler_params=pltpu.CompilerParams(
            collective_id=0, has_side_effects=True, vmem_limit_bytes=FRONT_MIB * 1024 * 1024
        ),
    )(*place(
        fine_nodes, mid_nodes, edge_receiver[0], edge_self[0], fine_edges.reshape(fanout, places, feature),
        node_self[0], edge_sender[0], jnp.swapaxes(fine_links, 1, 2), jnp.swapaxes(mid_links, 1, 2),
        coarse_links.reshape(fanout * crows, ccols), edge_bias, node_bias,
        coarse_edges.reshape(fanout * coarse_places, feature), mid_edges.reshape(fanout * mrows, mcols, feature),
        edge_output[0], node_output[0], node_summed[0], pooling[0], prolongation[0],
    ))
    front = list(front)
    front[0] = front[0].reshape(places, feature)
    front[15] = front[15].reshape(-1, hidden)
    front = [pltpu.with_memory_space_constraint(array, pltpu.VMEM) for array in front]
    length = fanout * BLOCK * cols
    coarse_rows = fanout * coarse_places if fanout * coarse_places <= length else coarse_places
    fine_out, fine_e, mid_out, mid_e, coarse_out, coarse_e = pl.pallas_call(
        functools.partial(update_kernel, fanout, across, along, ccols),
        name="update",
        in_specs=[vmem] * 29,
        out_shape=(
            struct((places, feature), BF16),
            struct((fanout, places, feature), BF16),
            struct((mrows, mcols, feature), BF16),
            struct((fanout * mrows, mcols, feature), BF16),
            struct((coarse_places, feature), BF16),
            struct((fanout * coarse_places, feature), BF16),
        ),
        out_specs=[anywhere] * 6,
        scratch_shapes=[
            pltpu.VMEM((2 if fanout * coarse_places <= length else 1, 2 * length, hidden), BF16),
            pltpu.VMEM((fanout, places, feature), BF16),
            pltpu.VMEM((places, feature), BF16),
            pltpu.VMEM((places, feature), BF16),
            pltpu.VMEM((places, feature), BF16),
            pltpu.VMEM((fanout * mid_places, hidden), BF16),
            pltpu.VMEM((fanout * mid_places, feature), F32),
            pltpu.VMEM((mrows, mcols, feature), BF16),
            pltpu.VMEM((fanout * mrows, mcols, feature), BF16),
            pltpu.VMEM((coarse_rows, hidden), BF16),
            pltpu.VMEM((coarse_places, feature), BF16),
            pltpu.VMEM((fanout * coarse_places, feature), BF16),
            pltpu.SemaphoreType.DMA((16,)),
        ],
        compiler_params=pltpu.CompilerParams(vmem_limit_bytes=(18 if fanout * coarse_places <= length else 20) * 1024 * 1024),
    )(
        *front, coarse_nodes.reshape(coarse_places, feature), edge_bias, node_bias, edge_gain, edge_shift,
        node_gain, node_shift,
    )
    return (
        fine_out.reshape(fine_nodes.shape),
        fine_e.reshape(fine_edges.shape),
        mid_out.reshape(mid_nodes.shape),
        mid_e.reshape(mid_edges.shape),
        coarse_out.reshape(coarse_nodes.shape),
        coarse_e.reshape(coarse_edges.shape),
    )


FRONT_MIB = 11


def solution(mesh):
    tile = P("dx", "dy", None)
    edge_tile = P(None, "dx", "dy", None)
    link_tile = P(None, "dx", "dy")
    return jax.shard_map(
        per_device,
        mesh=mesh,
        in_specs=(tile, edge_tile, link_tile) * 2 + (P(),) * 18,
        out_specs=(tile, edge_tile, tile, edge_tile, P(), P()),
        check_vma=False,
    )
```

```python
import functools

import jax
import jax.numpy as jnp
from jax import lax
from jax.experimental import pallas as pl
from jax.experimental.pallas import tpu as pltpu
from jax.sharding import PartitionSpec as P

FINE_REACH = 3
MID_REACH = 1
BLOCK = 4
epsilon = 1e-05
F32 = jnp.float32
BF16 = jnp.bfloat16
I32 = jnp.int32


def round_up(value, unit):
    return -(-value // unit) * unit


def dot(a, b):
    return jnp.dot(a, b, preferred_element_type=F32)


def spread(values, length):
    lines, width = values.shape
    row = lax.broadcasted_iota(I32, (length, lines), 0)
    line = lax.broadcasted_iota(I32, (length, lines), 1) * width
    owner = jnp.where((row >= line) & (row < line + width), 1.0, 0.0).astype(BF16)
    rows = dot(owner, values.astype(BF16))
    row = lax.broadcasted_iota(I32, (length, width), 0)
    lane = lax.broadcasted_iota(I32, (length, width), 1)
    return jnp.sum(jnp.where(lax.rem(row, width) == lane, rows, 0.0), axis=1, keepdims=True)


def chosen(column, width):
    lane = lax.broadcasted_iota(I32, (column.shape[0], width), 1).astype(column.dtype)
    return jnp.where(column == lane, 1.0, 0.0).astype(BF16)


def front_kernel(
    across, along,
    x_hbm, mid_hbm, wrec_hbm, ws_hbm, e_hbm, ns_hbm, wsend_hbm, links_hbm, mid_links_hbm, coarse_links_hbm,
    ebias_hbm, nbias_hbm, ce_hbm, me_hbm, wo_hbm, no_hbm, nsum_hbm, pool_hbm, prol_hbm,
    x_ref, wrec_ref, e_ref, ns_ref, wsend_ref, woc_ref, noc_ref, nsum_ref, pool_ref, prol_ref, ce_ref,
    zf_ref, zc_ref, zm_ref, xns_ref, terms_ref, pick_ref, pickm_ref, pickc_ref, me_ref, midpad_ref, pooled_ref,
    mid_ref, ws_ref, links_ref, mid_links_ref, coarse_links_ref, ebias_ref, nbias_ref, mid_e_ref, wo_ref, no_ref,
    receivers, halo,
    to_left, to_right, corner_src, top, bottom, from_left, from_right, corner_dst,
    mid_src, mid_rows_dst, mid_left, mid_right, mid_corner, pools,
    load_sem, near_send, near_recv, pool_send, pool_recv, far_send, far_recv,
):
    rows, cols, feature = x_ref.shape
    mrows, mcols, _ = mid_ref.shape
    fanout, places, hidden = zf_ref.shape
    half = rows // 2
    reach = FINE_REACH
    stride = cols + 8
    me_x = lax.axis_index("dx")
    me_y = lax.axis_index("dy")
    up = lax.rem(me_x + across - 1, across)
    down = lax.rem(me_x + 1, across)
    left = lax.rem(me_y + along - 1, along)
    right = lax.rem(me_y + 1, along)

    def beside_y(step):
        return me_x, lax.rem(me_y + step, along)

    def beside_x(step):
        return lax.rem(me_x + step, across), me_y

    group = fanout // 2
    loads = (
        (mid_hbm, mid_ref), (x_hbm, x_ref), (wrec_hbm, wrec_ref), (ebias_hbm, ebias_ref), (ws_hbm, ws_ref),
        (e_hbm.at[pl.ds(0, group)], e_ref.at[pl.ds(0, group)]),
        (e_hbm.at[pl.ds(group, group)], e_ref.at[pl.ds(group, group)]),
        (ns_hbm, ns_ref), (nbias_hbm, nbias_ref), (wsend_hbm, wsend_ref),
        (links_hbm, links_ref), (mid_links_hbm, mid_links_ref), (coarse_links_hbm, coarse_links_ref),
        (ce_hbm, ce_ref), (me_hbm, mid_e_ref), (wo_hbm, wo_ref), (no_hbm, no_ref), (nsum_hbm, nsum_ref),
        (pool_hbm, pool_ref), (prol_hbm, prol_ref),
    )
    loads = [pltpu.make_async_copy(source, target, load_sem.at[n]) for n, (source, target) in enumerate(loads)]
    (l_mid, l_x, l_wrec, l_ebias, l_ws, l_e0, l_e1, l_ns, l_nbias, l_wsend, l_links, l_mlinks, l_clinks,
     l_ce, l_me, l_wo, l_no, l_nsum, l_pool, l_prol) = loads
    for load in loads:
        load.start()

    barrier = pltpu.get_barrier_semaphore()

    def greet(device):
        pl.semaphore_signal(barrier, inc=1, device_id=device, device_id_type=pl.DeviceIdType.MESH)

    for step in range(1, along):
        greet(beside_y(step))
    for step in range(1, across):
        greet(beside_x(step))
    for device in ((down, right), (down, left), (up, right), (up, left)):
        greet(device)

    l_mid.wait()
    mid = mid_ref[...].astype(F32)
    brows, bcols = mrows // 4, mcols // 4
    means = []
    for i in range(brows):
        strip = jnp.sum(mid[4 * i : 4 * i + 4], axis=0)
        for j in range(bcols):
            means.append(jnp.sum(strip[4 * j : 4 * j + 4], axis=0, keepdims=True) * (1.0 / 16.0))
    pools[0, 0] = jnp.concatenate(means, axis=0).astype(BF16)
    mid_src[0] = jnp.concatenate([mid[i, mcols - 1 : mcols] for i in range(mrows)], axis=0).astype(BF16)
    mid_src[1] = jnp.concatenate([mid[i, 0:1] for i in range(mrows)], axis=0).astype(BF16)

    l_x.wait()
    l_wrec.wait()
    l_ebias.wait()
    low = lax.broadcasted_iota(I32, (half, 8, feature), 1) < 4
    first_a = x_ref[0:half, 0:8].astype(F32)
    first_b = x_ref[half:rows, 0:8].astype(F32)
    to_left[...] = jnp.where(low, first_a, pltpu.roll(first_b, 4, 1)).astype(BF16)
    last_a = x_ref[0:half, cols - 8 : cols].astype(F32)
    last_b = x_ref[half:rows, cols - 8 : cols].astype(F32)
    to_right[...] = jnp.where(low, pltpu.roll(last_a, 4, 1), last_b).astype(BF16)
    corner_src[0] = x_ref[rows - reach : rows, cols - 8 : cols]
    corner_src[1] = x_ref[rows - reach : rows, 0:8]
    corner_src[2] = x_ref[0:reach, cols - 8 : cols]
    corner_src[3] = x_ref[0:reach, 0:8]

    chunk = 512
    lanes = lambda c: slice(c * chunk, (c + 1) * chunk)
    chunks = range(hidden // chunk)
    light = []

    def beside(number):
        for _ in range(min(number, len(light))):
            light.pop(0)()

    for c in chunks:
        flat = x_ref[...].reshape(places, feature)
        receivers[:, lanes(c)] = (dot(flat, wrec_ref[:, lanes(c)]) + ebias_ref[:, lanes(c)]) * 0.5

    def own_edges(first, columns):
        for c in columns:
            beside(3)
            edges = e_ref[first : first + group].reshape(group * places, feature)
            z = dot(edges, ws_ref[:, lanes(c)]) * 0.5
            z = z.reshape(group, places, chunk) + receivers[:, lanes(c)][None]
            zf_ref[first : first + group, :, lanes(c)] = z.astype(zf_ref.dtype)

    l_ws.wait()
    l_e0.wait()
    own_edges(0, chunks[:1])

    pl.semaphore_wait(barrier, along + across + 2)

    line_copies = []
    for step in range(1, along):
        copy = pltpu.make_async_remote_copy(
            src_ref=pools.at[0, 0], dst_ref=pools.at[0, step], send_sem=pool_send.at[step],
            recv_sem=pool_recv.at[step], device_id=beside_y(step), device_id_type=pl.DeviceIdType.MESH,
        )
        copy.start()
        line_copies.append(copy)

    plan = (
        (to_right, from_left, (me_x, right)),
        (to_left, from_right, (me_x, left)),
        (x_ref.at[pl.ds(rows - reach, reach)], top, (down, me_y)),
        (x_ref.at[pl.ds(0, reach)], bottom, (up, me_y)),
        (corner_src.at[0], corner_dst.at[0], (down, right)),
        (corner_src.at[1], corner_dst.at[1], (down, left)),
        (corner_src.at[2], corner_dst.at[2], (up, right)),
        (corner_src.at[3], corner_dst.at[3], (up, left)),
        (mid_src.at[0], mid_left, (me_x, right)),
        (mid_src.at[1], mid_right, (me_x, left)),
        (mid_ref.at[mrows - 1], mid_rows_dst.at[0], (down, me_y)),
        (mid_ref.at[0], mid_rows_dst.at[1], (up, me_y)),
        (mid_ref.at[mrows - 1], mid_corner.at[0], (down, right)),
        (mid_ref.at[mrows - 1], mid_corner.at[1], (down, left)),
        (mid_ref.at[0], mid_corner.at[2], (up, right)),
        (mid_ref.at[0], mid_corner.at[3], (up, left)),
    )
    copies = []
    far_copies = []
    for number, (source, target, device) in enumerate(plan):
        copy = pltpu.make_async_remote_copy(
            src_ref=source, dst_ref=target, send_sem=near_send.at[number],
            recv_sem=near_recv.at[number], device_id=device, device_id_type=pl.DeviceIdType.MESH,
        )
        copy.start()
        copies.append(copy)


    own_edges(0, chunks[1:])

    l_e1.wait()
    l_ns.wait()
    l_nbias.wait()
    l_wsend.wait()
    l_ce.wait()
    l_me.wait()
    rem, div = lax.rem, lax.div
    l_links.wait()
    links = links_ref[...]
    span = 2 * FINE_REACH + 1
    column = lax.broadcasted_iota(I32, links.shape, 1) + rem(links, span) + (stride - FINE_REACH)
    line = rem(lax.broadcasted_iota(I32, links.shape, 2), BLOCK) + div(links, span)
    index = line * stride + rem(column, stride)
    window = pick_ref.shape[1]
    lane = lax.broadcasted_iota(I32, (cols, window), 1)

    def pick_block(s):
        for k in range(fanout):
            for i in range(BLOCK):
                x = s * BLOCK + i
                hit = jnp.where(index[k, :, x : x + 1] == lane, 1.0, 0.0).astype(BF16)
                begin = ((s * fanout + k) * BLOCK + i) * cols
                pick_ref[begin : begin + cols, :] = hit


    mid_places = mrows * mcols
    l_mlinks.wait()
    l_clinks.wait()

    def pick_mid():
        links = mid_links_ref[...]
        line = lax.broadcasted_iota(I32, links.shape, 2) + div(links, 3) - 1
        column = lax.broadcasted_iota(I32, links.shape, 1) + rem(links, 3) - 1
        centre = jnp.where(
            line < 0, mid_places + column,
            jnp.where(line >= mrows, mid_places + mcols + column, line * mcols + column),
        )
        side = mid_places + 2 * mcols + (line + 1) * mcols
        number = jnp.where(column < 0, side + mcols - 1, jnp.where(column >= mcols, side + (mrows + 2) * mcols, centre))
        mid_total = pickm_ref.shape[1]
        lane = lax.broadcasted_iota(I32, (mcols, mid_total), 1)
        for k in range(fanout):
            for x in range(0, mrows, 4):
                pieces = [jnp.where(number[k, :, x + i : x + i + 1] == lane, 1.0, 0.0) for i in range(4)]
                begin = (k * mrows + x) * mcols
                pickm_ref[begin : begin + 4 * mcols, :] = jnp.concatenate(pieces, axis=0).astype(BF16)

    def pick_coarse():
        count = pickc_ref.shape[0]
        pickc_ref[...] = chosen(spread(coarse_links_ref[...].astype(F32), count), pickc_ref.shape[1])

    def start_pads():
        midpad_ref[...] = jnp.zeros(midpad_ref.shape, F32)
        for i in range(mrows):
            midpad_ref[i * mcols : (i + 1) * mcols, :] = mid[i]
        terms_ref[rows + 2 * reach] = jnp.zeros((stride, hidden), BF16)

    light += [functools.partial(pick_block, s) for s in range(rows // BLOCK)]
    light += [pick_coarse, pick_mid, start_pads]
    l_wo.wait()
    l_no.wait()

    def centre_block(source, target, start):
        values = source[start : start + 256, :].astype(F32)
        target[start : start + 256, :] = (values - jnp.mean(values, axis=1, keepdims=True)).astype(BF16)

    for start in range(0, hidden, 256):
        light.append(functools.partial(centre_block, wo_ref, woc_ref, start))
        light.append(functools.partial(centre_block, no_ref, noc_ref, start))

    own_edges(group, chunks)

    for copy in line_copies:
        copy.wait()
    for step in range(1, across):
        copy = pltpu.make_async_remote_copy(
            src_ref=pools.at[0], dst_ref=pools.at[step], send_sem=far_send.at[step],
            recv_sem=far_recv.at[step], device_id=beside_x(step), device_id_type=pl.DeviceIdType.MESH,
        )
        copy.start()
        far_copies.append(copy)


    for c in chunks:
        beside(2)
        flat = x_ref[...].reshape(places, feature)
        own = (dot(flat, ns_ref[:, lanes(c)]) + nbias_ref[:, lanes(c)]) * 0.5
        xns_ref[:, lanes(c)] = own.astype(xns_ref.dtype)
        own = (dot(flat, wsend_ref[:, lanes(c)]) * 0.5).astype(BF16)
        terms_ref[reach : reach + rows, 0:cols, lanes(c)] = own.reshape(rows, cols, chunk)

    for i in range(fanout * mrows):
        me_ref[i * mcols : (i + 1) * mcols, :] = mid_e_ref[i].astype(F32)

    for c in chunks:
        beside(3)
        zc_ref[:, lanes(c)] = (dot(ce_ref[...], ws_ref[:, lanes(c)]) * 0.5).astype(zc_ref.dtype)
        zm_ref[:, lanes(c)] = (dot(me_ref[...].astype(BF16), ws_ref[:, lanes(c)]) * 0.5).astype(zm_ref.dtype)

    beside(len(light))
    for copy in copies:
        copy.wait()
    for load in (l_nsum, l_pool, l_prol):
        load.wait()

    for copy in far_copies:
        copy.wait()

    low3 = lax.broadcasted_iota(I32, (reach, 8, feature), 1) < 4
    above = jnp.where(low3, corner_dst[1].astype(F32), corner_dst[0].astype(F32)).astype(BF16)
    below = jnp.where(low3, corner_dst[3].astype(F32), corner_dst[2].astype(F32)).astype(BF16)
    for i in range(reach):
        for base, rows_of, corner in ((0, top, above), (reach, bottom, below)):
            begin = (base + i) * stride
            halo[begin : begin + cols, :] = rows_of[i]
            halo[begin + cols : begin + stride, :] = corner[i]
    fr = from_right[...].astype(F32)
    fl = from_left[...].astype(F32)
    beside = 2 * reach * stride
    middle = beside + half * 8
    halo[beside:middle, :] = jnp.where(low, fr, pltpu.roll(fl, 4, 1)).astype(BF16).reshape(half * 8, feature)
    halo[middle : middle + half * 8, :] = (
        jnp.where(low, pltpu.roll(fr, 4, 1), fl).astype(BF16).reshape(half * 8, feature)
    )

    base = mrows * mcols
    midpad_ref[base : base + mcols, :] = mid_rows_dst[0].astype(F32)
    midpad_ref[base + mcols : base + 2 * mcols, :] = mid_rows_dst[1].astype(F32)
    for side, (tile, above, below, seat) in enumerate(((mid_left, 0, 2, mcols - 1), (mid_right, 1, 3, 0))):
        start = base + 2 * mcols + side * (mrows + 2) * mcols
        midpad_ref[start : start + mcols, :] = mid_corner[above].astype(F32)
        values = tile[...].astype(F32)
        for i in range(mrows):
            place = start + (i + 1) * mcols + seat
            midpad_ref[place : place + 1, :] = values[i : i + 1]
        finish = start + (mrows + 1) * mcols
        midpad_ref[finish : finish + mcols, :] = mid_corner[below].astype(F32)

    count = brows * bcols
    for step in range(across):
        for slot in range(along):
            begin = (step * along + slot) * count
            pooled_ref[begin : begin + count, :] = pools[step, slot].astype(F32)

    for c in chunks:
        far = (dot(halo[...], wsend_ref[:, lanes(c)]) * 0.5).astype(BF16)
        deep = reach * stride
        terms_ref[0:reach, :, lanes(c)] = far[0:deep].reshape(reach, stride, chunk)
        terms_ref[reach + rows : rows + 2 * reach, :, lanes(c)] = far[deep : 2 * deep].reshape(reach, stride, chunk)
        terms_ref[reach : reach + rows, cols:stride, lanes(c)] = far[2 * deep :].reshape(rows, 8, chunk)


def update_kernel(
    fanout, across, along, coarse_cols,
    x_ref, wrec_ref, e_ref, ns_ref, wsend_ref, wo_ref, no_ref, nsum_ref, pool_ref, prol_ref, ce_ref,
    zf_ref, zc_ref, zm_ref, xns_ref, terms_ref, pick_ref, pickm_ref, pickc_ref, me_ref, midpad_ref, pooled_ref,
    coarse_ref, ebias_ref, nbias_ref, egain_ref, eshift_ref, ngain_ref, nshift_ref,
    x_out, e_out, mid_out, mid_e_out, coarse_out, coarse_e_out,
    act, e_new, summed, x_new, mid_act, mid_flat, mid_new, mid_e_new, coarse_act, coarse_new, coarse_e_new,
    sems,
):
    places, feature = x_ref.shape
    hidden = wrec_ref.shape[1]
    chunk = 512
    mrows, mcols, _ = mid_new.shape
    mid_places = mrows * mcols
    coarse_places = coarse_ref.shape[0]
    cols = mcols * 4
    rows = places // cols
    stride = cols + 8
    window = pick_ref.shape[1]
    block = BLOCK * cols
    length = fanout * block
    pair = 2
    steps = rows // (BLOCK * pair)
    cuts = [slice(start, start + chunk) for start in range(0, hidden, chunk)]
    started = []

    def send(source, target):
        copy = pltpu.make_async_copy(source, target, sems.at[len(started)])
        copy.start()
        started.append(copy)

    def silu_half(values):
        small = values.astype(BF16)
        return small + small * jnp.tanh(small)

    def scaled(values, gain, shift):
        variance = jnp.mean(values * values, axis=-1, keepdims=True)
        return values * lax.rsqrt(variance + epsilon) * gain[...] + shift[...]

    def gather(step, sub):
        number = step * pair + sub
        here = slice(number * block, (number + 1) * block)
        begin = number * BLOCK * stride
        mine = pick_ref[number * length : (number + 1) * length, :]
        slot = step % act.shape[0]
        for cut in cuts:
            z = dot(mine, terms_ref[begin : begin + window, cut])
            z = z + zf_ref[:, here, cut].reshape(length, chunk).astype(F32)
            act[slot, sub * length : (sub + 1) * length, cut] = silu_half(z)

    def message(step):
        values = scaled(dot(act[step % act.shape[0]], wo_ref[...]), egain_ref, eshift_ref)
        for sub in range(pair):
            number = step * pair + sub
            here = slice(number * block, (number + 1) * block)
            part = values[sub * length : (sub + 1) * length].reshape(fanout, block, feature)
            new = e_ref[:, here, :].astype(F32) + part
            e_new[:, here, :] = new.astype(BF16)
            summed[here, :] = (jnp.sum(new, axis=0) * 0.5).astype(BF16)
        here = pl.ds(step * pair * block, pair * block)
        send(e_new.at[:, here, :], e_out.at[:, here, :])

    def node_hidden(own, incoming):
        return silu_half(own + dot(incoming, nsum_ref[...]))

    def node_final(nodes, inner):
        return nodes.astype(F32) + scaled(dot(inner, no_ref[...]), ngain_ref, nshift_ref)

    state = {}

    def coarse_start():
        me_x, me_y = lax.axis_index("dx"), lax.axis_index("dy")
        brows, bcols = mrows // 4, mcols // 4
        div, rem = lax.div, lax.rem
        row = lax.broadcasted_iota(I32, (coarse_places, 1), 0)
        line, column = div(row, coarse_cols), rem(row, coarse_cols)
        slot = rem(me_x + across - div(line, brows), across) * along + rem(me_y + along - div(column, bcols), along)
        place = chosen(slot * (brows * bcols) + rem(line, brows) * bcols + rem(column, bcols), coarse_places)
        pooled = dot(place, pooled_ref[...].astype(BF16)).astype(BF16)
        pre = (coarse_ref[...].astype(F32) + dot(pooled, pool_ref[...])).astype(BF16)
        state["pre"] = pre
        state["term"] = (dot(pre, wsend_ref[...]) * 0.5).astype(BF16)
        state["receiver"] = (dot(pre, wrec_ref[...]) + ebias_ref[...]) * 0.5
        state["own"] = (dot(pre, ns_ref[...]) + nbias_ref[...]) * 0.5

    together = fanout if fanout * coarse_places <= length else 1

    def coarse_part(first):
        span = slice(first * coarse_places, (first + together) * coarse_places)
        for cut in cuts:
            z = dot(pickc_ref[span, :], state["term"][:, cut]) + zc_ref[span, cut].astype(F32)
            z = z.reshape(together, coarse_places, chunk) + state["receiver"][:, cut][None]
            coarse_act[:, cut] = silu_half(z.reshape(together * coarse_places, chunk))

    def coarse_gather():
        coarse_part(0)

    def coarse_message():
        incoming = jnp.zeros((coarse_places, feature), F32)
        for first in range(0, fanout, together):
            span = slice(first * coarse_places, (first + together) * coarse_places)
            if first:
                coarse_part(first)
            new = ce_ref[span, :].astype(F32) + scaled(dot(coarse_act[...], wo_ref[...]), egain_ref, eshift_ref)
            coarse_e_new[span, :] = new.astype(BF16)
            incoming = incoming + jnp.sum(new.reshape(together, coarse_places, feature), axis=0)
        send(coarse_e_new, coarse_e_out)
        state["incoming"] = (incoming * 0.5).astype(BF16)

    def coarse_node():
        inner = node_hidden(state["own"], state["incoming"])
        coarse = node_final(state["pre"], inner).astype(BF16)
        coarse_new[...] = coarse
        send(coarse_new, coarse_out)
        state["coarse"] = coarse

    def mid_start():
        me_x, me_y = lax.axis_index("dx"), lax.axis_index("dy")
        div, rem = lax.div, lax.rem
        row = lax.broadcasted_iota(I32, (midpad_ref.shape[0], 1), 0)
        beside = row - mid_places - 2 * mcols
        deep = (mrows + 2) * mcols
        seat = jnp.maximum(beside, 0)
        line = jnp.where(
            row < mid_places, div(row, mcols),
            jnp.where(row < mid_places + mcols, -1, jnp.where(beside < 0, mrows, div(rem(seat, deep), mcols) - 1)),
        )
        column = jnp.where(beside < 0, rem(row, mcols), jnp.where(beside < deep, -1, mcols))
        line = rem(me_x * mrows + line + across * mrows, across * mrows)
        column = rem(me_y * mcols + column + along * mcols, along * mcols)
        parent = dot(chosen(div(line, 4) * coarse_cols + div(column, 4), coarse_places), state["coarse"]).astype(BF16)
        padded = (midpad_ref[...] + dot(parent, prol_ref[...])).astype(BF16)
        pre = padded[:mid_places]
        state["pre"] = pre
        state["term"] = (dot(padded, wsend_ref[...]) * 0.5).astype(BF16)
        state["receiver"] = (dot(pre, wrec_ref[...]) + ebias_ref[...]) * 0.5
        state["own"] = (dot(pre, ns_ref[...]) + nbias_ref[...]) * 0.5

    def mid_gather():
        for cut in cuts:
            z = dot(pickm_ref[...], state["term"][:, cut]) + zm_ref[:, cut].astype(F32)
            z = z.reshape(fanout, mid_places, chunk) + state["receiver"][:, cut][None]
            mid_act[:, cut] = silu_half(z.reshape(fanout * mid_places, chunk))

    def mid_message():
        new = me_ref[...] + scaled(dot(mid_act[...], wo_ref[...]), egain_ref, eshift_ref)
        mid_flat[...] = new
        for i in range(fanout * mrows):
            mid_e_new[i] = mid_flat[i * mcols : (i + 1) * mcols, :].astype(BF16)
        send(mid_e_new, mid_e_out)
        state["incoming"] = (jnp.sum(new.reshape(fanout, mid_places, feature), axis=0) * 0.5).astype(BF16)

    pending = [
        coarse_start, coarse_gather, coarse_message, coarse_node, mid_start, mid_gather, mid_message,
    ]

    def next_small():
        if pending:
            pending.pop(0)()

    next_small()
    for step in range(steps):
        for sub in range(pair):
            gather(step, sub)
        next_small()
        message(step)
        next_small()
    while pending:
        next_small()
    own = jnp.concatenate([state["own"], xns_ref[...].astype(F32)], axis=0)
    inner = node_hidden(own, jnp.concatenate([state["incoming"], summed[...]], axis=0))
    fresh = node_final(jnp.concatenate([state["pre"], x_ref[...]], axis=0), inner)
    mid = fresh[:mid_places].astype(BF16)
    fresh = fresh[mid_places:]
    values = mid.astype(F32)
    for i in range(mrows):
        mid_new[i] = values[i * mcols : (i + 1) * mcols].astype(BF16)
    send(mid_new, mid_out)
    lifted = dot(mid, prol_ref[...])
    for a in range(mrows):
        group = [
            jnp.broadcast_to(lifted[a * mcols + b : a * mcols + b + 1], (4, feature)) for b in range(mcols)
        ]
        lift = jnp.concatenate(group * 4, axis=0)
        here = slice(a * 4 * cols, (a + 1) * 4 * cols)
        x_new[here, :] = (fresh[here, :].astype(BF16).astype(F32) + lift).astype(BF16)
        here = pl.ds(a * 4 * cols, 4 * cols)
        send(x_new.at[here, :], x_out.at[here, :])
    for copy in started:
        copy.wait()


def per_device(
    fine_nodes, fine_edges, fine_links, mid_nodes, mid_edges, mid_links, coarse_nodes, coarse_edges,
    coarse_links, edge_self, edge_sender, edge_receiver, edge_bias, edge_output, edge_gain, edge_shift,
    node_self, node_summed, node_bias, node_output, node_gain, node_shift, prolongation, pooling,
):
    rows, cols, feature = fine_nodes.shape
    mrows, mcols, _ = mid_nodes.shape
    crows, ccols, _ = coarse_nodes.shape
    fanout = fine_edges.shape[0]
    across, along = lax.axis_size("dx"), lax.axis_size("dy")
    total = across * along
    places, mid_places, coarse_places = rows * cols, mrows * mcols, crows * ccols
    count = (mrows // 4) * (mcols // 4)
    stride = cols + 8
    hidden = edge_self.shape[2]
    window = round_up((BLOCK + 2 * FINE_REACH) * stride, 256)
    mid_total = round_up(3 * (mrows + 2) * mcols, 128)
    reach = FINE_REACH
    wide = BF16
    fuller = F32 if coarse_places * fanout <= places else BF16

    anywhere = pl.BlockSpec(memory_space=pl.ANY)
    vmem = pl.BlockSpec(memory_space=pltpu.VMEM)
    struct = jax.ShapeDtypeStruct
    fine_tile = pltpu.VMEM((rows, cols, feature), BF16)
    weight_in = pltpu.VMEM((feature, hidden), BF16)
    weight_out = pltpu.VMEM((hidden, feature), BF16)
    square = pltpu.VMEM((feature, feature), BF16)
    place = lambda *arrays: [pltpu.with_memory_space_constraint(array, pltpu.HBM) for array in arrays]
    front = pl.pallas_call(
        functools.partial(front_kernel, across, along),
        name="front",
        in_specs=[pl.BlockSpec(memory_space=pltpu.HBM)] * 19,
        out_shape=(
            fine_tile, weight_in, pltpu.VMEM((fanout, places, feature), BF16), weight_in, weight_in, weight_out, weight_out,
            weight_in, square, square, pltpu.VMEM((fanout * coarse_places, feature), BF16),
            pltpu.VMEM((fanout, places, hidden), wide), pltpu.VMEM((fanout * coarse_places, hidden), wide),
            pltpu.VMEM((fanout * mid_places, hidden), fuller), pltpu.VMEM((places, hidden), fuller),
            pltpu.VMEM((rows + 2 * reach + 1, stride, hidden), BF16), pltpu.VMEM((fanout * places, window), BF16),
            pltpu.VMEM((fanout * mid_places, mid_total), BF16), pltpu.VMEM((fanout * coarse_places, coarse_places), BF16),
            pltpu.VMEM((fanout * mid_places, feature), F32), pltpu.VMEM((mid_total, feature), F32),
            pltpu.VMEM((total * count, feature), F32),
        ),
        out_specs=[vmem] * 22,
        scratch_shapes=[
            pltpu.VMEM((mrows, mcols, feature), BF16),
            pltpu.VMEM((feature, hidden), BF16),
            pltpu.VMEM((fanout, cols, rows), I32),
            pltpu.VMEM((fanout, mcols, mrows), I32),
            pltpu.VMEM((fanout * crows, ccols), I32),
            pltpu.VMEM((1, hidden), F32),
            pltpu.VMEM((1, hidden), F32),
            pltpu.VMEM((fanout * mrows, mcols, feature), BF16),
            pltpu.VMEM((hidden, feature), BF16),
            pltpu.VMEM((hidden, feature), BF16),
            pltpu.VMEM((places, hidden), F32),
            pltpu.VMEM((2 * reach * stride + rows * 8, feature), BF16),
            pltpu.VMEM((rows // 2, 8, feature), BF16),
            pltpu.VMEM((rows // 2, 8, feature), BF16),
            pltpu.VMEM((4, reach, 8, feature), BF16),
            pltpu.VMEM((reach, cols, feature), BF16),
            pltpu.VMEM((reach, cols, feature), BF16),
            pltpu.VMEM((rows // 2, 8, feature), BF16),
            pltpu.VMEM((rows // 2, 8, feature), BF16),
            pltpu.VMEM((4, reach, 8, feature), BF16),
            pltpu.VMEM((2, mrows, feature), BF16),
            pltpu.VMEM((2, mcols, feature), BF16),
            pltpu.VMEM((mrows, feature), BF16),
            pltpu.VMEM((mrows, feature), BF16),
            pltpu.VMEM((4, mcols, feature), BF16),
            pltpu.VMEM((across, along, count, feature), BF16),
            pltpu.SemaphoreType.DMA((20,)),
            pltpu.SemaphoreType.DMA((16,)),
            pltpu.SemaphoreType.DMA((16,)),
            pltpu.SemaphoreType.DMA((along,)),
            pltpu.SemaphoreType.DMA((along,)),
            pltpu.SemaphoreType.DMA((across,)),
            pltpu.SemaphoreType.DMA((across,)),
        ],
        compiler_params=pltpu.CompilerParams(
            collective_id=0, has_side_effects=True, vmem_limit_bytes=FRONT_MIB * 1024 * 1024
        ),
    )(*place(
        fine_nodes, mid_nodes, edge_receiver[0], edge_self[0], fine_edges.reshape(fanout, places, feature),
        node_self[0], edge_sender[0], jnp.swapaxes(fine_links, 1, 2), jnp.swapaxes(mid_links, 1, 2),
        coarse_links.reshape(fanout * crows, ccols), edge_bias, node_bias,
        coarse_edges.reshape(fanout * coarse_places, feature), mid_edges.reshape(fanout * mrows, mcols, feature),
        edge_output[0], node_output[0], node_summed[0], pooling[0], prolongation[0],
    ))
    front = list(front)
    front[0] = front[0].reshape(places, feature)
    front[15] = front[15].reshape(-1, hidden)
    front = [pltpu.with_memory_space_constraint(array, pltpu.VMEM) for array in front]
    length = fanout * BLOCK * cols
    coarse_rows = fanout * coarse_places if fanout * coarse_places <= length else coarse_places
    fine_out, fine_e, mid_out, mid_e, coarse_out, coarse_e = pl.pallas_call(
        functools.partial(update_kernel, fanout, across, along, ccols),
        name="update",
        in_specs=[vmem] * 29,
        out_shape=(
            struct((places, feature), BF16),
            struct((fanout, places, feature), BF16),
            struct((mrows, mcols, feature), BF16),
            struct((fanout * mrows, mcols, feature), BF16),
            struct((coarse_places, feature), BF16),
            struct((fanout * coarse_places, feature), BF16),
        ),
        out_specs=[anywhere] * 6,
        scratch_shapes=[
            pltpu.VMEM((2 if fanout * coarse_places <= length else 1, 2 * length, hidden), BF16),
            pltpu.VMEM((fanout, places, feature), BF16),
            pltpu.VMEM((places, feature), BF16),
            pltpu.VMEM((places, feature), BF16),
            pltpu.VMEM((fanout * mid_places, hidden), BF16),
            pltpu.VMEM((fanout * mid_places, feature), F32),
            pltpu.VMEM((mrows, mcols, feature), BF16),
            pltpu.VMEM((fanout * mrows, mcols, feature), BF16),
            pltpu.VMEM((coarse_rows, hidden), BF16),
            pltpu.VMEM((coarse_places, feature), BF16),
            pltpu.VMEM((fanout * coarse_places, feature), BF16),
            pltpu.SemaphoreType.DMA((rows // BLOCK + rows // 8 + 8,)),
        ],
        compiler_params=pltpu.CompilerParams(vmem_limit_bytes=(18 if fanout * coarse_places <= length else 20) * 1024 * 1024),
    )(
        *front, coarse_nodes.reshape(coarse_places, feature), edge_bias, node_bias, edge_gain, edge_shift,
        node_gain, node_shift,
    )
    return (
        fine_out.reshape(fine_nodes.shape),
        fine_e.reshape(fine_edges.shape),
        mid_out.reshape(mid_nodes.shape),
        mid_e.reshape(mid_edges.shape),
        coarse_out.reshape(coarse_nodes.shape),
        coarse_e.reshape(coarse_edges.shape),
    )


FRONT_MIB = 11


def solution(mesh):
    tile = P("dx", "dy", None)
    edge_tile = P(None, "dx", "dy", None)
    link_tile = P(None, "dx", "dy")
    return jax.shard_map(
        per_device,
        mesh=mesh,
        in_specs=(tile, edge_tile, link_tile) * 2 + (P(),) * 18,
        out_specs=(tile, edge_tile, tile, edge_tile, P(), P()),
        check_vma=False,
    )
```

```python
import functools

import jax
import jax.numpy as jnp
from jax import lax
from jax.experimental import pallas as pl
from jax.experimental.pallas import tpu as pltpu
from jax.sharding import PartitionSpec as P

FINE_REACH = 3
MID_REACH = 1
BLOCK = 4
epsilon = 1e-05
F32 = jnp.float32
BF16 = jnp.bfloat16
I32 = jnp.int32


def round_up(value, unit):
    return -(-value // unit) * unit


def dot(a, b):
    return jnp.dot(a, b, preferred_element_type=F32)


def spread(values, length):
    lines, width = values.shape
    row = lax.broadcasted_iota(I32, (length, lines), 0)
    line = lax.broadcasted_iota(I32, (length, lines), 1) * width
    owner = jnp.where((row >= line) & (row < line + width), 1.0, 0.0).astype(BF16)
    rows = dot(owner, values.astype(BF16))
    row = lax.broadcasted_iota(I32, (length, width), 0)
    lane = lax.broadcasted_iota(I32, (length, width), 1)
    return jnp.sum(jnp.where(lax.rem(row, width) == lane, rows, 0.0), axis=1, keepdims=True)


def chosen(column, width):
    lane = lax.broadcasted_iota(I32, (column.shape[0], width), 1).astype(column.dtype)
    return jnp.where(column == lane, 1.0, 0.0).astype(BF16)


def front_kernel(
    across, along,
    x_hbm, mid_hbm, wrec_hbm, ws_hbm, e_hbm, ns_hbm, wsend_hbm, links_hbm, mid_links_hbm, coarse_links_hbm,
    ebias_hbm, nbias_hbm, ce_hbm, me_hbm, wo_hbm, no_hbm, nsum_hbm, pool_hbm, prol_hbm,
    x_ref, wrec_ref, e_ref, ns_ref, wsend_ref, woc_ref, noc_ref, nsum_ref, pool_ref, prol_ref, ce_ref,
    zf_ref, zc_ref, zm_ref, xns_ref, terms_ref, pick_ref, pickm_ref, pickc_ref, me_ref, midpad_ref, pooled_ref,
    mid_ref, ws_ref, links_ref, mid_links_ref, coarse_links_ref, ebias_ref, nbias_ref, mid_e_ref, wo_ref, no_ref,
    receivers, halo,
    to_left, to_right, corner_src, top, bottom, from_left, from_right, corner_dst,
    mid_src, mid_rows_dst, mid_left, mid_right, mid_corner, pools,
    load_sem, near_send, near_recv, pool_send, pool_recv, far_send, far_recv,
):
    rows, cols, feature = x_ref.shape
    mrows, mcols, _ = mid_ref.shape
    fanout, places, hidden = zf_ref.shape
    half = rows // 2
    reach = FINE_REACH
    stride = cols + 8
    me_x = lax.axis_index("dx")
    me_y = lax.axis_index("dy")
    up = lax.rem(me_x + across - 1, across)
    down = lax.rem(me_x + 1, across)
    left = lax.rem(me_y + along - 1, along)
    right = lax.rem(me_y + 1, along)

    def beside_y(step):
        return me_x, lax.rem(me_y + step, along)

    def beside_x(step):
        return lax.rem(me_x + step, across), me_y

    barrier = pltpu.get_barrier_semaphore()

    def greet(device):
        pl.semaphore_signal(barrier, inc=1, device_id=device, device_id_type=pl.DeviceIdType.MESH)

    for step in range(1, along):
        greet(beside_y(step))
    for step in range(1, across):
        greet(beside_x(step))
    for device in ((down, right), (down, left), (up, right), (up, left)):
        greet(device)

    group = fanout // 2
    loads = (
        (mid_hbm, mid_ref), (x_hbm, x_ref), (wrec_hbm, wrec_ref), (ebias_hbm, ebias_ref), (ws_hbm, ws_ref),
        (e_hbm.at[pl.ds(0, group)], e_ref.at[pl.ds(0, group)]),
        (e_hbm.at[pl.ds(group, group)], e_ref.at[pl.ds(group, group)]),
        (ns_hbm, ns_ref), (nbias_hbm, nbias_ref), (wsend_hbm, wsend_ref),
        (links_hbm, links_ref), (mid_links_hbm, mid_links_ref), (coarse_links_hbm, coarse_links_ref),
        (ce_hbm, ce_ref), (me_hbm, mid_e_ref), (wo_hbm, wo_ref), (no_hbm, no_ref), (nsum_hbm, nsum_ref),
        (pool_hbm, pool_ref), (prol_hbm, prol_ref),
    )
    loads = [pltpu.make_async_copy(source, target, load_sem.at[n]) for n, (source, target) in enumerate(loads)]
    (l_mid, l_x, l_wrec, l_ebias, l_ws, l_e0, l_e1, l_ns, l_nbias, l_wsend, l_links, l_mlinks, l_clinks,
     l_ce, l_me, l_wo, l_no, l_nsum, l_pool, l_prol) = loads
    for load in loads:
        load.start()

    l_mid.wait()
    mid = mid_ref[...].astype(F32)
    brows, bcols = mrows // 4, mcols // 4
    means = []
    for i in range(brows):
        strip = jnp.sum(mid[4 * i : 4 * i + 4], axis=0)
        for j in range(bcols):
            means.append(jnp.sum(strip[4 * j : 4 * j + 4], axis=0, keepdims=True) * (1.0 / 16.0))
    pools[0, 0] = jnp.concatenate(means, axis=0).astype(BF16)
    mid_src[0] = jnp.concatenate([mid[i, mcols - 1 : mcols] for i in range(mrows)], axis=0).astype(BF16)
    mid_src[1] = jnp.concatenate([mid[i, 0:1] for i in range(mrows)], axis=0).astype(BF16)

    l_x.wait()
    l_wrec.wait()
    l_ebias.wait()
    low = lax.broadcasted_iota(I32, (half, 8, feature), 1) < 4
    first_a = x_ref[0:half, 0:8].astype(F32)
    first_b = x_ref[half:rows, 0:8].astype(F32)
    to_left[...] = jnp.where(low, first_a, pltpu.roll(first_b, 4, 1)).astype(BF16)
    last_a = x_ref[0:half, cols - 8 : cols].astype(F32)
    last_b = x_ref[half:rows, cols - 8 : cols].astype(F32)
    to_right[...] = jnp.where(low, pltpu.roll(last_a, 4, 1), last_b).astype(BF16)
    corner_src[0] = x_ref[rows - reach : rows, cols - 8 : cols]
    corner_src[1] = x_ref[rows - reach : rows, 0:8]
    corner_src[2] = x_ref[0:reach, cols - 8 : cols]
    corner_src[3] = x_ref[0:reach, 0:8]

    chunk = 512
    lanes = lambda c: slice(c * chunk, (c + 1) * chunk)
    chunks = range(hidden // chunk)
    light = []

    def beside(number):
        for _ in range(min(number, len(light))):
            light.pop(0)()

    for c in chunks:
        flat = x_ref[...].reshape(places, feature)
        receivers[:, lanes(c)] = (dot(flat, wrec_ref[:, lanes(c)]) + ebias_ref[:, lanes(c)]) * 0.5

    def own_edges(first, columns):
        for c in columns:
            beside(3)
            edges = e_ref[first : first + group].reshape(group * places, feature)
            z = dot(edges, ws_ref[:, lanes(c)]) * 0.5
            z = z.reshape(group, places, chunk) + receivers[:, lanes(c)][None]
            zf_ref[first : first + group, :, lanes(c)] = z.astype(zf_ref.dtype)

    pl.semaphore_wait(barrier, along + across + 2)

    line_copies = []
    for step in range(1, along):
        copy = pltpu.make_async_remote_copy(
            src_ref=pools.at[0, 0], dst_ref=pools.at[0, step], send_sem=pool_send.at[step],
            recv_sem=pool_recv.at[step], device_id=beside_y(step), device_id_type=pl.DeviceIdType.MESH,
        )
        copy.start()
        line_copies.append(copy)

    plan = (
        (to_right, from_left, (me_x, right)),
        (to_left, from_right, (me_x, left)),
        (x_ref.at[pl.ds(rows - reach, reach)], top, (down, me_y)),
        (x_ref.at[pl.ds(0, reach)], bottom, (up, me_y)),
        (corner_src.at[0], corner_dst.at[0], (down, right)),
        (corner_src.at[1], corner_dst.at[1], (down, left)),
        (corner_src.at[2], corner_dst.at[2], (up, right)),
        (corner_src.at[3], corner_dst.at[3], (up, left)),
        (mid_src.at[0], mid_left, (me_x, right)),
        (mid_src.at[1], mid_right, (me_x, left)),
        (mid_ref.at[mrows - 1], mid_rows_dst.at[0], (down, me_y)),
        (mid_ref.at[0], mid_rows_dst.at[1], (up, me_y)),
        (mid_ref.at[mrows - 1], mid_corner.at[0], (down, right)),
        (mid_ref.at[mrows - 1], mid_corner.at[1], (down, left)),
        (mid_ref.at[0], mid_corner.at[2], (up, right)),
        (mid_ref.at[0], mid_corner.at[3], (up, left)),
    )
    copies = []
    far_copies = []
    for number, (source, target, device) in enumerate(plan):
        copy = pltpu.make_async_remote_copy(
            src_ref=source, dst_ref=target, send_sem=near_send.at[number],
            recv_sem=near_recv.at[number], device_id=device, device_id_type=pl.DeviceIdType.MESH,
        )
        copy.start()
        copies.append(copy)


    l_ws.wait()
    l_e0.wait()
    own_edges(0, chunks[:1])

    own_edges(0, chunks[1:])

    l_e1.wait()
    l_ns.wait()
    l_nbias.wait()
    l_wsend.wait()
    l_ce.wait()
    l_me.wait()
    rem, div = lax.rem, lax.div
    l_links.wait()
    links = links_ref[...]
    span = 2 * FINE_REACH + 1
    column = lax.broadcasted_iota(I32, links.shape, 1) + rem(links, span) + (stride - FINE_REACH)
    line = rem(lax.broadcasted_iota(I32, links.shape, 2), BLOCK) + div(links, span)
    index = line * stride + rem(column, stride)
    window = pick_ref.shape[1]
    lane = lax.broadcasted_iota(I32, (cols, window), 1)

    def pick_block(s):
        for k in range(fanout):
            for i in range(BLOCK):
                x = s * BLOCK + i
                hit = jnp.where(index[k, :, x : x + 1] == lane, 1.0, 0.0).astype(BF16)
                begin = ((s * fanout + k) * BLOCK + i) * cols
                pick_ref[begin : begin + cols, :] = hit


    mid_places = mrows * mcols
    l_mlinks.wait()
    l_clinks.wait()

    def pick_mid():
        links = mid_links_ref[...]
        line = lax.broadcasted_iota(I32, links.shape, 2) + div(links, 3) - 1
        column = lax.broadcasted_iota(I32, links.shape, 1) + rem(links, 3) - 1
        centre = jnp.where(
            line < 0, mid_places + column,
            jnp.where(line >= mrows, mid_places + mcols + column, line * mcols + column),
        )
        side = mid_places + 2 * mcols + (line + 1) * mcols
        number = jnp.where(column < 0, side + mcols - 1, jnp.where(column >= mcols, side + (mrows + 2) * mcols, centre))
        mid_total = pickm_ref.shape[1]
        lane = lax.broadcasted_iota(I32, (mcols, mid_total), 1)
        for k in range(fanout):
            for x in range(0, mrows, 4):
                pieces = [jnp.where(number[k, :, x + i : x + i + 1] == lane, 1.0, 0.0) for i in range(4)]
                begin = (k * mrows + x) * mcols
                pickm_ref[begin : begin + 4 * mcols, :] = jnp.concatenate(pieces, axis=0).astype(BF16)

    def pick_coarse():
        count = pickc_ref.shape[0]
        pickc_ref[...] = chosen(spread(coarse_links_ref[...].astype(F32), count), pickc_ref.shape[1])

    def start_pads():
        midpad_ref[...] = jnp.zeros(midpad_ref.shape, F32)
        for i in range(mrows):
            midpad_ref[i * mcols : (i + 1) * mcols, :] = mid[i]
        terms_ref[rows + 2 * reach] = jnp.zeros((stride, hidden), BF16)

    light += [functools.partial(pick_block, s) for s in range(rows // BLOCK)]
    light += [pick_coarse, pick_mid, start_pads]
    l_wo.wait()
    l_no.wait()

    def centre_block(source, target, start):
        values = source[start : start + 256, :].astype(F32)
        target[start : start + 256, :] = (values - jnp.mean(values, axis=1, keepdims=True)).astype(BF16)

    for start in range(0, hidden, 256):
        light.append(functools.partial(centre_block, wo_ref, woc_ref, start))
        light.append(functools.partial(centre_block, no_ref, noc_ref, start))

    own_edges(group, chunks)

    for copy in line_copies:
        copy.wait()
    for step in range(1, across):
        copy = pltpu.make_async_remote_copy(
            src_ref=pools.at[0], dst_ref=pools.at[step], send_sem=far_send.at[step],
            recv_sem=far_recv.at[step], device_id=beside_x(step), device_id_type=pl.DeviceIdType.MESH,
        )
        copy.start()
        far_copies.append(copy)


    for c in chunks:
        beside(2)
        flat = x_ref[...].reshape(places, feature)
        own = (dot(flat, ns_ref[:, lanes(c)]) + nbias_ref[:, lanes(c)]) * 0.5
        xns_ref[:, lanes(c)] = own.astype(xns_ref.dtype)
        own = (dot(flat, wsend_ref[:, lanes(c)]) * 0.5).astype(BF16)
        terms_ref[reach : reach + rows, 0:cols, lanes(c)] = own.reshape(rows, cols, chunk)

    for i in range(fanout * mrows):
        me_ref[i * mcols : (i + 1) * mcols, :] = mid_e_ref[i].astype(F32)

    for c in chunks:
        beside(3)
        zc_ref[:, lanes(c)] = (dot(ce_ref[...], ws_ref[:, lanes(c)]) * 0.5).astype(zc_ref.dtype)
        zm_ref[:, lanes(c)] = (dot(me_ref[...].astype(BF16), ws_ref[:, lanes(c)]) * 0.5).astype(zm_ref.dtype)

    beside(len(light))
    for copy in copies:
        copy.wait()
    for load in (l_nsum, l_pool, l_prol):
        load.wait()

    for copy in far_copies:
        copy.wait()

    low3 = lax.broadcasted_iota(I32, (reach, 8, feature), 1) < 4
    above = jnp.where(low3, corner_dst[1].astype(F32), corner_dst[0].astype(F32)).astype(BF16)
    below = jnp.where(low3, corner_dst[3].astype(F32), corner_dst[2].astype(F32)).astype(BF16)
    for i in range(reach):
        for base, rows_of, corner in ((0, top, above), (reach, bottom, below)):
            begin = (base + i) * stride
            halo[begin : begin + cols, :] = rows_of[i]
            halo[begin + cols : begin + stride, :] = corner[i]
    fr = from_right[...].astype(F32)
    fl = from_left[...].astype(F32)
    beside = 2 * reach * stride
    middle = beside + half * 8
    halo[beside:middle, :] = jnp.where(low, fr, pltpu.roll(fl, 4, 1)).astype(BF16).reshape(half * 8, feature)
    halo[middle : middle + half * 8, :] = (
        jnp.where(low, pltpu.roll(fr, 4, 1), fl).astype(BF16).reshape(half * 8, feature)
    )

    base = mrows * mcols
    midpad_ref[base : base + mcols, :] = mid_rows_dst[0].astype(F32)
    midpad_ref[base + mcols : base + 2 * mcols, :] = mid_rows_dst[1].astype(F32)
    for side, (tile, above, below, seat) in enumerate(((mid_left, 0, 2, mcols - 1), (mid_right, 1, 3, 0))):
        start = base + 2 * mcols + side * (mrows + 2) * mcols
        midpad_ref[start : start + mcols, :] = mid_corner[above].astype(F32)
        values = tile[...].astype(F32)
        for i in range(mrows):
            place = start + (i + 1) * mcols + seat
            midpad_ref[place : place + 1, :] = values[i : i + 1]
        finish = start + (mrows + 1) * mcols
        midpad_ref[finish : finish + mcols, :] = mid_corner[below].astype(F32)

    count = brows * bcols
    for step in range(across):
        for slot in range(along):
            begin = (step * along + slot) * count
            pooled_ref[begin : begin + count, :] = pools[step, slot].astype(F32)

    for c in chunks:
        far = (dot(halo[...], wsend_ref[:, lanes(c)]) * 0.5).astype(BF16)
        deep = reach * stride
        terms_ref[0:reach, :, lanes(c)] = far[0:deep].reshape(reach, stride, chunk)
        terms_ref[reach + rows : rows + 2 * reach, :, lanes(c)] = far[deep : 2 * deep].reshape(reach, stride, chunk)
        terms_ref[reach : reach + rows, cols:stride, lanes(c)] = far[2 * deep :].reshape(rows, 8, chunk)


def update_kernel(
    fanout, across, along, coarse_cols,
    x_ref, wrec_ref, e_ref, ns_ref, wsend_ref, wo_ref, no_ref, nsum_ref, pool_ref, prol_ref, ce_ref,
    zf_ref, zc_ref, zm_ref, xns_ref, terms_ref, pick_ref, pickm_ref, pickc_ref, me_ref, midpad_ref, pooled_ref,
    coarse_ref, ebias_ref, nbias_ref, egain_ref, eshift_ref, ngain_ref, nshift_ref,
    x_out, e_out, mid_out, mid_e_out, coarse_out, coarse_e_out,
    act, e_new, summed, x_new, mid_act, mid_flat, mid_new, mid_e_new, coarse_act, coarse_new, coarse_e_new,
    sems,
):
    places, feature = x_ref.shape
    hidden = wrec_ref.shape[1]
    chunk = 512
    mrows, mcols, _ = mid_new.shape
    mid_places = mrows * mcols
    coarse_places = coarse_ref.shape[0]
    cols = mcols * 4
    rows = places // cols
    stride = cols + 8
    window = pick_ref.shape[1]
    block = BLOCK * cols
    length = fanout * block
    pair = 2
    steps = rows // (BLOCK * pair)
    cuts = [slice(start, start + chunk) for start in range(0, hidden, chunk)]
    started = []

    def send(source, target):
        copy = pltpu.make_async_copy(source, target, sems.at[len(started)])
        copy.start()
        started.append(copy)

    def silu_half(values):
        small = values.astype(BF16)
        return small + small * jnp.tanh(small)

    def scaled(values, gain, shift):
        variance = jnp.mean(values * values, axis=-1, keepdims=True)
        return values * lax.rsqrt(variance + epsilon) * gain[...] + shift[...]

    def gather(step, sub):
        number = step * pair + sub
        here = slice(number * block, (number + 1) * block)
        begin = number * BLOCK * stride
        mine = pick_ref[number * length : (number + 1) * length, :]
        slot = step % act.shape[0]
        for cut in cuts:
            z = dot(mine, terms_ref[begin : begin + window, cut])
            z = z + zf_ref[:, here, cut].reshape(length, chunk).astype(F32)
            act[slot, sub * length : (sub + 1) * length, cut] = silu_half(z)

    def message(step):
        values = scaled(dot(act[step % act.shape[0]], wo_ref[...]), egain_ref, eshift_ref)
        for sub in range(pair):
            number = step * pair + sub
            here = slice(number * block, (number + 1) * block)
            part = values[sub * length : (sub + 1) * length].reshape(fanout, block, feature)
            new = e_ref[:, here, :].astype(F32) + part
            e_new[:, here, :] = new.astype(BF16)
            summed[here, :] = (jnp.sum(new, axis=0) * 0.5).astype(BF16)
        here = pl.ds(step * pair * block, pair * block)
        send(e_new.at[:, here, :], e_out.at[:, here, :])

    def node_hidden(own, incoming):
        return silu_half(own + dot(incoming, nsum_ref[...]))

    def node_final(nodes, inner):
        return nodes.astype(F32) + scaled(dot(inner, no_ref[...]), ngain_ref, nshift_ref)

    state = {}

    def coarse_start():
        me_x, me_y = lax.axis_index("dx"), lax.axis_index("dy")
        brows, bcols = mrows // 4, mcols // 4
        div, rem = lax.div, lax.rem
        row = lax.broadcasted_iota(I32, (coarse_places, 1), 0)
        line, column = div(row, coarse_cols), rem(row, coarse_cols)
        slot = rem(me_x + across - div(line, brows), across) * along + rem(me_y + along - div(column, bcols), along)
        place = chosen(slot * (brows * bcols) + rem(line, brows) * bcols + rem(column, bcols), coarse_places)
        pooled = dot(place, pooled_ref[...].astype(BF16)).astype(BF16)
        pre = (coarse_ref[...].astype(F32) + dot(pooled, pool_ref[...])).astype(BF16)
        state["pre"] = pre
        state["term"] = (dot(pre, wsend_ref[...]) * 0.5).astype(BF16)
        state["receiver"] = (dot(pre, wrec_ref[...]) + ebias_ref[...]) * 0.5
        state["own"] = (dot(pre, ns_ref[...]) + nbias_ref[...]) * 0.5

    together = fanout if fanout * coarse_places <= length else 1

    def coarse_part(first):
        span = slice(first * coarse_places, (first + together) * coarse_places)
        for cut in cuts:
            z = dot(pickc_ref[span, :], state["term"][:, cut]) + zc_ref[span, cut].astype(F32)
            z = z.reshape(together, coarse_places, chunk) + state["receiver"][:, cut][None]
            coarse_act[:, cut] = silu_half(z.reshape(together * coarse_places, chunk))

    def coarse_gather():
        coarse_part(0)

    def coarse_message():
        incoming = jnp.zeros((coarse_places, feature), F32)
        for first in range(0, fanout, together):
            span = slice(first * coarse_places, (first + together) * coarse_places)
            if first:
                coarse_part(first)
            new = ce_ref[span, :].astype(F32) + scaled(dot(coarse_act[...], wo_ref[...]), egain_ref, eshift_ref)
            coarse_e_new[span, :] = new.astype(BF16)
            incoming = incoming + jnp.sum(new.reshape(together, coarse_places, feature), axis=0)
        send(coarse_e_new, coarse_e_out)
        state["incoming"] = (incoming * 0.5).astype(BF16)

    def coarse_node():
        inner = node_hidden(state["own"], state["incoming"])
        coarse = node_final(state["pre"], inner).astype(BF16)
        coarse_new[...] = coarse
        send(coarse_new, coarse_out)
        state["coarse"] = coarse

    def mid_start():
        me_x, me_y = lax.axis_index("dx"), lax.axis_index("dy")
        div, rem = lax.div, lax.rem
        row = lax.broadcasted_iota(I32, (midpad_ref.shape[0], 1), 0)
        beside = row - mid_places - 2 * mcols
        deep = (mrows + 2) * mcols
        seat = jnp.maximum(beside, 0)
        line = jnp.where(
            row < mid_places, div(row, mcols),
            jnp.where(row < mid_places + mcols, -1, jnp.where(beside < 0, mrows, div(rem(seat, deep), mcols) - 1)),
        )
        column = jnp.where(beside < 0, rem(row, mcols), jnp.where(beside < deep, -1, mcols))
        line = rem(me_x * mrows + line + across * mrows, across * mrows)
        column = rem(me_y * mcols + column + along * mcols, along * mcols)
        parent = dot(chosen(div(line, 4) * coarse_cols + div(column, 4), coarse_places), state["coarse"]).astype(BF16)
        padded = (midpad_ref[...] + dot(parent, prol_ref[...])).astype(BF16)
        pre = padded[:mid_places]
        state["pre"] = pre
        state["term"] = (dot(padded, wsend_ref[...]) * 0.5).astype(BF16)
        state["receiver"] = (dot(pre, wrec_ref[...]) + ebias_ref[...]) * 0.5
        state["own"] = (dot(pre, ns_ref[...]) + nbias_ref[...]) * 0.5

    def mid_gather():
        for cut in cuts:
            z = dot(pickm_ref[...], state["term"][:, cut]) + zm_ref[:, cut].astype(F32)
            z = z.reshape(fanout, mid_places, chunk) + state["receiver"][:, cut][None]
            mid_act[:, cut] = silu_half(z.reshape(fanout * mid_places, chunk))

    def mid_message():
        new = me_ref[...] + scaled(dot(mid_act[...], wo_ref[...]), egain_ref, eshift_ref)
        mid_flat[...] = new
        for i in range(fanout * mrows):
            mid_e_new[i] = mid_flat[i * mcols : (i + 1) * mcols, :].astype(BF16)
        send(mid_e_new, mid_e_out)
        state["incoming"] = (jnp.sum(new.reshape(fanout, mid_places, feature), axis=0) * 0.5).astype(BF16)

    pending = [
        coarse_start, coarse_gather, coarse_message, coarse_node, mid_start, mid_gather, mid_message,
    ]

    def next_small():
        if pending:
            pending.pop(0)()

    next_small()
    for step in range(steps):
        for sub in range(pair):
            gather(step, sub)
        next_small()
        message(step)
        next_small()
    while pending:
        next_small()
    own = jnp.concatenate([state["own"], xns_ref[...].astype(F32)], axis=0)
    inner = node_hidden(own, jnp.concatenate([state["incoming"], summed[...]], axis=0))
    fresh = node_final(jnp.concatenate([state["pre"], x_ref[...]], axis=0), inner)
    mid = fresh[:mid_places].astype(BF16)
    fresh = fresh[mid_places:]
    values = mid.astype(F32)
    for i in range(mrows):
        mid_new[i] = values[i * mcols : (i + 1) * mcols].astype(BF16)
    send(mid_new, mid_out)
    lifted = dot(mid, prol_ref[...])
    for a in range(mrows):
        group = [
            jnp.broadcast_to(lifted[a * mcols + b : a * mcols + b + 1], (4, feature)) for b in range(mcols)
        ]
        lift = jnp.concatenate(group * 4, axis=0)
        here = slice(a * 4 * cols, (a + 1) * 4 * cols)
        x_new[here, :] = (fresh[here, :].astype(BF16).astype(F32) + lift).astype(BF16)
        here = pl.ds(a * 4 * cols, 4 * cols)
        send(x_new.at[here, :], x_out.at[here, :])
    for copy in started:
        copy.wait()


def per_device(
    fine_nodes, fine_edges, fine_links, mid_nodes, mid_edges, mid_links, coarse_nodes, coarse_edges,
    coarse_links, edge_self, edge_sender, edge_receiver, edge_bias, edge_output, edge_gain, edge_shift,
    node_self, node_summed, node_bias, node_output, node_gain, node_shift, prolongation, pooling,
):
    rows, cols, feature = fine_nodes.shape
    mrows, mcols, _ = mid_nodes.shape
    crows, ccols, _ = coarse_nodes.shape
    fanout = fine_edges.shape[0]
    across, along = lax.axis_size("dx"), lax.axis_size("dy")
    total = across * along
    places, mid_places, coarse_places = rows * cols, mrows * mcols, crows * ccols
    count = (mrows // 4) * (mcols // 4)
    stride = cols + 8
    hidden = edge_self.shape[2]
    window = round_up((BLOCK + 2 * FINE_REACH) * stride, 256)
    mid_total = round_up(3 * (mrows + 2) * mcols, 128)
    reach = FINE_REACH
    wide = BF16
    fuller = F32 if coarse_places * fanout <= places else BF16

    anywhere = pl.BlockSpec(memory_space=pl.ANY)
    vmem = pl.BlockSpec(memory_space=pltpu.VMEM)
    struct = jax.ShapeDtypeStruct
    fine_tile = pltpu.VMEM((rows, cols, feature), BF16)
    weight_in = pltpu.VMEM((feature, hidden), BF16)
    weight_out = pltpu.VMEM((hidden, feature), BF16)
    square = pltpu.VMEM((feature, feature), BF16)
    place = lambda *arrays: [pltpu.with_memory_space_constraint(array, pltpu.HBM) for array in arrays]
    front = pl.pallas_call(
        functools.partial(front_kernel, across, along),
        name="front",
        in_specs=[pl.BlockSpec(memory_space=pltpu.HBM)] * 19,
        out_shape=(
            fine_tile, weight_in, pltpu.VMEM((fanout, places, feature), BF16), weight_in, weight_in, weight_out, weight_out,
            weight_in, square, square, pltpu.VMEM((fanout * coarse_places, feature), BF16),
            pltpu.VMEM((fanout, places, hidden), wide), pltpu.VMEM((fanout * coarse_places, hidden), wide),
            pltpu.VMEM((fanout * mid_places, hidden), fuller), pltpu.VMEM((places, hidden), fuller),
            pltpu.VMEM((rows + 2 * reach + 1, stride, hidden), BF16), pltpu.VMEM((fanout * places, window), BF16),
            pltpu.VMEM((fanout * mid_places, mid_total), BF16), pltpu.VMEM((fanout * coarse_places, coarse_places), BF16),
            pltpu.VMEM((fanout * mid_places, feature), F32), pltpu.VMEM((mid_total, feature), F32),
            pltpu.VMEM((total * count, feature), F32),
        ),
        out_specs=[vmem] * 22,
        scratch_shapes=[
            pltpu.VMEM((mrows, mcols, feature), BF16),
            pltpu.VMEM((feature, hidden), BF16),
            pltpu.VMEM((fanout, cols, rows), I32),
            pltpu.VMEM((fanout, mcols, mrows), I32),
            pltpu.VMEM((fanout * crows, ccols), I32),
            pltpu.VMEM((1, hidden), F32),
            pltpu.VMEM((1, hidden), F32),
            pltpu.VMEM((fanout * mrows, mcols, feature), BF16),
            pltpu.VMEM((hidden, feature), BF16),
            pltpu.VMEM((hidden, feature), BF16),
            pltpu.VMEM((places, hidden), F32),
            pltpu.VMEM((2 * reach * stride + rows * 8, feature), BF16),
            pltpu.VMEM((rows // 2, 8, feature), BF16),
            pltpu.VMEM((rows // 2, 8, feature), BF16),
            pltpu.VMEM((4, reach, 8, feature), BF16),
            pltpu.VMEM((reach, cols, feature), BF16),
            pltpu.VMEM((reach, cols, feature), BF16),
            pltpu.VMEM((rows // 2, 8, feature), BF16),
            pltpu.VMEM((rows // 2, 8, feature), BF16),
            pltpu.VMEM((4, reach, 8, feature), BF16),
            pltpu.VMEM((2, mrows, feature), BF16),
            pltpu.VMEM((2, mcols, feature), BF16),
            pltpu.VMEM((mrows, feature), BF16),
            pltpu.VMEM((mrows, feature), BF16),
            pltpu.VMEM((4, mcols, feature), BF16),
            pltpu.VMEM((across, along, count, feature), BF16),
            pltpu.SemaphoreType.DMA((20,)),
            pltpu.SemaphoreType.DMA((16,)),
            pltpu.SemaphoreType.DMA((16,)),
            pltpu.SemaphoreType.DMA((along,)),
            pltpu.SemaphoreType.DMA((along,)),
            pltpu.SemaphoreType.DMA((across,)),
            pltpu.SemaphoreType.DMA((across,)),
        ],
        compiler_params=pltpu.CompilerParams(
            collective_id=0, has_side_effects=True, vmem_limit_bytes=FRONT_MIB * 1024 * 1024
        ),
    )(*place(
        fine_nodes, mid_nodes, edge_receiver[0], edge_self[0], fine_edges.reshape(fanout, places, feature),
        node_self[0], edge_sender[0], jnp.swapaxes(fine_links, 1, 2), jnp.swapaxes(mid_links, 1, 2),
        coarse_links.reshape(fanout * crows, ccols), edge_bias, node_bias,
        coarse_edges.reshape(fanout * coarse_places, feature), mid_edges.reshape(fanout * mrows, mcols, feature),
        edge_output[0], node_output[0], node_summed[0], pooling[0], prolongation[0],
    ))
    front = list(front)
    front[0] = front[0].reshape(places, feature)
    front[15] = front[15].reshape(-1, hidden)
    front = [pltpu.with_memory_space_constraint(array, pltpu.VMEM) for array in front]
    length = fanout * BLOCK * cols
    coarse_rows = fanout * coarse_places if fanout * coarse_places <= length else coarse_places
    fine_out, fine_e, mid_out, mid_e, coarse_out, coarse_e = pl.pallas_call(
        functools.partial(update_kernel, fanout, across, along, ccols),
        name="update",
        in_specs=[vmem] * 29,
        out_shape=(
            struct((places, feature), BF16),
            struct((fanout, places, feature), BF16),
            struct((mrows, mcols, feature), BF16),
            struct((fanout * mrows, mcols, feature), BF16),
            struct((coarse_places, feature), BF16),
            struct((fanout * coarse_places, feature), BF16),
        ),
        out_specs=[anywhere] * 6,
        scratch_shapes=[
            pltpu.VMEM((2 if fanout * coarse_places <= length else 1, 2 * length, hidden), BF16),
            pltpu.VMEM((fanout, places, feature), BF16),
            pltpu.VMEM((places, feature), BF16),
            pltpu.VMEM((places, feature), BF16),
            pltpu.VMEM((fanout * mid_places, hidden), BF16),
            pltpu.VMEM((fanout * mid_places, feature), F32),
            pltpu.VMEM((mrows, mcols, feature), BF16),
            pltpu.VMEM((fanout * mrows, mcols, feature), BF16),
            pltpu.VMEM((coarse_rows, hidden), BF16),
            pltpu.VMEM((coarse_places, feature), BF16),
            pltpu.VMEM((fanout * coarse_places, feature), BF16),
            pltpu.SemaphoreType.DMA((rows // BLOCK + rows // 8 + 8,)),
        ],
        compiler_params=pltpu.CompilerParams(vmem_limit_bytes=(18 if fanout * coarse_places <= length else 20) * 1024 * 1024),
    )(
        *front, coarse_nodes.reshape(coarse_places, feature), edge_bias, node_bias, edge_gain, edge_shift,
        node_gain, node_shift,
    )
    return (
        fine_out.reshape(fine_nodes.shape),
        fine_e.reshape(fine_edges.shape),
        mid_out.reshape(mid_nodes.shape),
        mid_e.reshape(mid_edges.shape),
        coarse_out.reshape(coarse_nodes.shape),
        coarse_e.reshape(coarse_edges.shape),
    )


FRONT_MIB = 11


def solution(mesh):
    tile = P("dx", "dy", None)
    edge_tile = P(None, "dx", "dy", None)
    link_tile = P(None, "dx", "dy")
    return jax.shard_map(
        per_device,
        mesh=mesh,
        in_specs=(tile, edge_tile, link_tile) * 2 + (P(),) * 18,
        out_specs=(tile, edge_tile, tile, edge_tile, P(), P()),
        check_vma=False,
    )
```
